128 devices in a mesh: lang: 4 (over y), seq: 32 (over x, z, core).
Axes of the slice: x: 4, y: 4, z: 4, core: 2. Of those that a mesh axis runs over, the one named last changes fastest.
Arguments:
- q_stream: bfloat16 [4, 4096, 4096], P('lang', 'seq'), may hold values from -6 to 6
- k_stream: bfloat16 [4, 4096, 4096], P('lang', 'seq'), may hold values from -6 to 6
- v_stream: bfloat16 [4, 4096, 4096], P('lang', 'seq'), may hold values from -6 to 6
- lang_ids: int32 [4, 64], P('lang', 'seq'), may hold values from 0 to 15
- short_taps: bfloat16 [16, 3, 3, 4096], P('lang'), may hold values from -4 to 4
- adapter_down: bfloat16 [16, 16, 4096], P('lang'), may hold values from -0.09375 to 0.09375
- adapter_up: bfloat16 [16, 16, 4096], P('lang'), may hold values from -1.5 to 1.5
- long_filter: float32 [4096, 4096], P(None, 'seq'), as said below
- bypass_coefficient: float32 [4096], replicated, may hold values from 0.5 to 1.5
Outputs:
- output: bfloat16 [4, 4096, 4096], P('lang', 'seq')
The draws below stay inside these ranges and needn't reach their ends.
Inputs may be any that keep to these rules, and one draw needn't show every extreme that they name: `long_filter`: each channel's filter may be rough in the lag.
All inputs are finite; a program needn't handle non-finite values.
Results may differ from the reference program's by a relative error of at most 0.009.
Values may be sent and summed in bfloat16 or wider, within the bound.
A program may use at most 128 MiB of HBM per device.

```python
import math
import jax
import jax.numpy as jnp
import numpy as np

MODEL_DIM = 4096
R = 16
SEG_DEV = 2
SEQS = 4
SEQUENCE_SPAN = 4096
LANGS = 16
N_SEQ = 32


def draw_long_filter(key, part):
    key_rows = jax.random.split(jax.random.fold_in(key, 7), 8)
    lag_offsets = jnp.arange(SEQUENCE_SPAN, dtype=jnp.float32)[:, None]
    slow_count = 5
    jitter = jax.random.normal(key_rows[0], (SEQUENCE_SPAN, MODEL_DIM), jnp.float32)
    tail_jitter = jax.random.normal(key_rows[6], (SEQUENCE_SPAN, MODEL_DIM), jnp.float32)
    slow_pick = jax.random.randint(key_rows[1], (MODEL_DIM,), 0, 10) < slow_count
    fast_rate = jnp.exp(jax.random.uniform(key_rows[2], (MODEL_DIM,), jnp.float32, math.log(1.0 / 50.0), math.log(1.0 / 30.0)))
    slow_rate = jnp.exp(jax.random.uniform(key_rows[3], (MODEL_DIM,), jnp.float32, math.log(0.1), math.log(2.0))) / SEQUENCE_SPAN
    tail_rate = jnp.exp(jax.random.uniform(key_rows[7], (MODEL_DIM,), jnp.float32, math.log(0.1), math.log(2.0))) / SEQUENCE_SPAN
    decay_rate = jnp.where(slow_pick, slow_rate, fast_rate)
    pulse_position = jax.random.randint(key_rows[4], (3, MODEL_DIM), 0, SEQUENCE_SPAN)
    scale_factor = jnp.ones((SEQUENCE_SPAN, MODEL_DIM), jnp.float32)
    for pulse_signal in range(3):
        scale_factor = scale_factor * jnp.where(lag_offsets >= pulse_position[pulse_signal][None, :].astype(jnp.float32), 0.6, 1.0)
    main_norm = jnp.sqrt(jnp.expm1(-2.0 * decay_rate) / jnp.expm1(-2.0 * decay_rate * SEQUENCE_SPAN))
    tail_norm = jnp.sqrt(jnp.expm1(-2.0 * tail_rate) / jnp.expm1(-2.0 * tail_rate * SEQUENCE_SPAN))
    main_part = jitter * jnp.exp(-decay_rate[None, :] * lag_offsets) * main_norm[None, :]
    tail_part = tail_jitter * jnp.exp(-tail_rate[None, :] * lag_offsets) * tail_norm[None, :]
    tail_share = jnp.where(slow_pick, 0.0, 0.25)
    combined = jnp.sqrt(1.0 - tail_share)[None, :] * main_part + jnp.sqrt(tail_share)[None, :] * tail_part
    return (combined * scale_factor).astype(jnp.float32)


def place_ends(values, own_key, low, high):
    index_at = [jax.random.randint(jax.random.fold_in(own_key, axis), (), 0, length) for axis, length in enumerate(values.shape)]
    main_axis = values.shape.index(max(values.shape))
    neighbour = index_at[:main_axis] + [(index_at[main_axis] + 1) % values.shape[main_axis]] + index_at[main_axis + 1:]
    return values.at[tuple(index_at)].set(low).at[tuple(neighbour)].set(high)


def block_levels(stream_key, dims, shards, smallest, largest):
    gain = 1.0
    for position, parts in shards:
        heights = jax.random.uniform(jax.random.fold_in(jax.random.fold_in(stream_key, 6), position), (parts,), jnp.float32, smallest / len(shards), largest / len(shards))
        gain = gain * jnp.repeat(jnp.exp(heights), dims[position] // parts).reshape((-1,) + (1,) * (len(dims) - 1 - position))
    return gain


def rank_table(number_of, skew):
    loads = [(1 << 20) // math.isqrt(grade ** skew) + 1 for grade in range(1, number_of + 1)]
    deviation = 1 + sum(loads) // (1 << 30)
    return np.cumsum(np.array([max(1, weight // deviation) for weight in loads]))


def skewed_ids(stream_key, extent, count, slope):
    listing = rank_table(count, slope)
    ticket = jax.random.randint(jax.random.fold_in(stream_key, 1), extent, 0, int(listing[count - 1]))
    standing = jnp.searchsorted(jnp.asarray(listing, jnp.int32), ticket, side="right")
    return jax.random.permutation(jax.random.fold_in(stream_key, 2), count)[standing].astype(jnp.int32)


def scatter_about(rng, extent, spread, reach, shards=(), kind=jnp.bfloat16):
    drawn = jax.random.normal(rng, extent, jnp.float32) * spread
    if len(shards) > 0:
        drawn = block_levels(rng, extent, shards, -0.22, 0.18) * drawn
    return jnp.clip(drawn, min=-reach, max=reach).astype(kind)


def setup_inputs(seed: int = 0) -> dict:
    key_list = jax.random.split(jax.random.key(seed), 10)
    return {
        "q_stream": scatter_about(key_list[0], (SEQS, SEQUENCE_SPAN, MODEL_DIM), 1.0, 6.0, ((0, 4), (1, 32))),
        "k_stream": scatter_about(key_list[1], (SEQS, SEQUENCE_SPAN, MODEL_DIM), 1.0, 6.0, ((0, 4), (1, 32))),
        "v_stream": scatter_about(key_list[2], (SEQS, SEQUENCE_SPAN, MODEL_DIM), 1.0, 6.0, ((0, 4), (1, 32))),
        "lang_ids": place_ends(skewed_ids(key_list[3], (SEQS, SEG_DEV * N_SEQ), LANGS, 2), jax.random.fold_in(key_list[3], 3), 0, LANGS - 1).astype(jnp.int32),
        "short_taps": scatter_about(key_list[4], (LANGS, 3, 3, MODEL_DIM), 0.6, 4.0, ((0, 4),)),
        "adapter_down": scatter_about(key_list[5], (LANGS, R, MODEL_DIM), MODEL_DIM ** -0.5, 0.09375, ((0, 4),)),
        "adapter_up": scatter_about(key_list[6], (LANGS, R, MODEL_DIM), R ** -0.5, 1.5, ((0, 4),)),
        "long_filter": draw_long_filter(jax.random.fold_in(key_list[9], 71), 0),
        "bypass_coefficient": jnp.clip(jax.random.uniform(key_list[8], (MODEL_DIM,), jnp.float32, 0.5, 1.5), 0.5, 1.5),
    }


def short_filter(data, short_taps, tok_lang, stream_index):
    timestep_count, model_channel_width = data.shape
    extended = jnp.concatenate([jnp.zeros((2, model_channel_width), data.dtype), data], 0)
    summed = jnp.zeros((timestep_count, model_channel_width), jnp.float32)
    for offset in range(3):
        weights = short_taps[:, offset, stream_index, :][tok_lang]
        summed = summed + extended[2 - offset:2 - offset + timestep_count].astype(jnp.float32) * weights.astype(jnp.float32)
    return summed


def reference(q_stream, k_stream, v_stream, lang_ids, short_taps, adapter_down, adapter_up, long_filter, bypass_coefficient):
    seq_count, timestep_count, model_channel_width = q_stream.shape
    seg_count = lang_ids.shape[1]
    seg_len = timestep_count // seg_count
    filt_spectrum = jnp.fft.rfft(long_filter.astype(jnp.float32), n=2 * timestep_count, axis=0)
    panel_entries_group = min(512, model_channel_width)
    results = []
    for which in range(seq_count):
        seg_lang = lang_ids[which]
        tok_lang = jnp.repeat(seg_lang, seg_len)
        qshort = short_filter(q_stream[which], short_taps, tok_lang, 0).astype(jnp.bfloat16)
        query_local_smoothed = short_filter(k_stream[which], short_taps, tok_lang, 1)
        payload_local_smoothed = short_filter(v_stream[which], short_taps, tok_lang, 2)
        modulating_cosine = (query_local_smoothed * payload_local_smoothed).astype(jnp.bfloat16)
        down_rows = adapter_down[seg_lang].astype(jnp.float32)
        up_rows = adapter_up[seg_lang].astype(jnp.float32)
        folded = qshort.reshape(seg_count, seg_len, model_channel_width).astype(jnp.float32)
        low = jnp.einsum("snd,srd->snr", folded, down_rows).astype(jnp.bfloat16)
        gate = qshort.astype(jnp.float32) + jnp.einsum("snr,srd->snd", low.astype(jnp.float32), up_rows).reshape(timestep_count, model_channel_width)
        modulation_rate = modulating_cosine.astype(jnp.float32)
        pieces = []
        for first_feature_index in range(0, model_channel_width, panel_entries_group):
            spectral_gain = jnp.fft.rfft(modulation_rate[:, first_feature_index:first_feature_index + panel_entries_group], n=2 * timestep_count, axis=0)
            product = spectral_gain * filt_spectrum[:, first_feature_index:first_feature_index + panel_entries_group]
            pieces.append(jnp.fft.irfft(product, n=2 * timestep_count, axis=0)[:timestep_count])
        long_filter_result = jnp.concatenate(pieces, 1).astype(jnp.float32)
        gated_combination = (long_filter_result + bypass_coefficient[None, :] * modulation_rate).astype(jnp.bfloat16)
        results.append((gate * gated_combination.astype(jnp.float32)).astype(jnp.bfloat16))
    return jnp.stack(results)
```

```python
import math

import jax
import jax.numpy as jnp
import ml_dtypes
import numpy as np
from jax import lax
from jax.experimental import pallas as pl
from jax.experimental.pallas import tpu as pltpu
from jax.sharding import PartitionSpec as P

LANES = 128
ROWS = 16


def shifted_2(x, axis, by):
    length = lax.axis_size(axis)
    pairs = [(i, i + by) for i in range(length) if 0 <= i + by < length]
    return lax.ppermute(x, axis, pairs)


def dft_tables():
    k1 = np.arange(512)[:, None]
    a = np.arange(512)[None, :]
    ang = 2.0 * np.pi * ((2 * k1 + 1) * a % 2048) / 2048.0
    table = np.concatenate([np.cos(ang), -np.sin(ang)], 0).astype(np.float32)
    one = 2.0 * np.pi * (2 * np.arange(512) + 1) / 16384.0
    step = np.stack([np.cos(one), -np.sin(one)]).astype(np.float32)
    step = np.ascontiguousarray(np.broadcast_to(step[:, :, None], (2, 512, LANES)))
    fwd = table.astype(ml_dtypes.bfloat16)
    return fwd, np.ascontiguousarray(fwd.T), step


def cadd(p, q):
    return p[0] + q[0], p[1] + q[1]


def csub(p, q):
    return p[0] - q[0], p[1] - q[1]


def cmul(p, q):
    return p[0] * q[0] - p[1] * q[1], p[0] * q[1] + p[1] * q[0]


def cmul_conj(p, q):
    return p[0] * q[0] + p[1] * q[1], p[1] * q[0] - p[0] * q[1]


def quarter(p, sign):
    return (p[1], -p[0]) if sign > 0 else (-p[1], p[0])


def dft4(z0, z1, z2, z3, sign):
    s0, s1 = cadd(z0, z2), csub(z0, z2)
    s2, s3 = cadd(z1, z3), quarter(csub(z1, z3), sign)
    return cadd(s0, s2), cadd(s1, s3), csub(s0, s2), csub(s1, s3)


def dft8(z, sign):
    half = math.sqrt(0.5)
    even = dft4(z[0], z[2], z[4], z[6], sign)
    odd = dft4(z[1], z[3], z[5], z[7], sign)
    o1, o3 = odd[1], odd[3]
    if sign > 0:
        o1 = ((o1[0] + o1[1]) * half, (o1[1] - o1[0]) * half)
        o3 = ((o3[1] - o3[0]) * half, (o3[0] + o3[1]) * -half)
    else:
        o1 = ((o1[0] - o1[1]) * half, (o1[0] + o1[1]) * half)
        o3 = ((o3[0] + o3[1]) * -half, (o3[0] - o3[1]) * half)
    turned = (odd[0], o1, quarter(odd[2], sign), o3)
    return [cadd(e, o) for e, o in zip(even, turned)] + [csub(e, o) for e, o in zip(even, turned)]


def lane(b):
    return slice(b * LANES, (b + 1) * LANES)


def stage_matmul(out_ref, left_ref, right_refs, width=256):
    columns = out_ref.shape[1]

    @pl.loop(0, columns // width)
    def _(j):
        cols = pl.ds(pl.multiple_of(j * width, width), width)
        total = None
        for right_ref in right_refs:
            term = jnp.dot(left_ref[...], right_ref[:, cols], preferred_element_type=jnp.float32)
            total = term if total is None else total + term
        out_ref[:, cols] = total


def load_points(p_ref, rows_re, rows_im):
    return [(p_ref[rows_re, lane(b)], p_ref[rows_im, lane(b)]) for b in range(8)]


def filter_spectrum(filt_ref, table_ref, step_ref, high_ref, low_ref, p_ref, h_ref, tw_ref):
    for b in range(8):
        @pl.loop(0, 4)
        def _(i):
            rows = filt_ref[pl.ds(i * 1024 + b, 128, stride=8), :]
            high = rows.astype(jnp.bfloat16)
            at = pl.ds(pl.multiple_of(i * 128, 128), 128)
            high_ref[at, lane(b)] = high
            low_ref[at, lane(b)] = (rows - high.astype(jnp.float32)).astype(jnp.bfloat16)
    stage_matmul(p_ref, table_ref, [high_ref, low_ref])

    @pl.loop(0, 512 // ROWS)
    def _(i):
        re = pl.ds(pl.multiple_of(i * ROWS, ROWS), ROWS)
        im = pl.ds(pl.multiple_of(512 + i * ROWS, ROWS), ROWS)
        points = load_points(p_ref, re, im)
        step = (step_ref[0, re, :], step_ref[1, re, :])
        turn = step
        for b in range(1, 8):
            tw_ref[re, lane(b)] = turn[0]
            tw_ref[im, lane(b)] = turn[1]
            points[b] = cmul(points[b], turn)
            if b < 7:
                turn = cmul(turn, step)
        for k2, value in enumerate(dft8(points, 1)):
            h_ref[re, lane(k2)] = value[0] * (2.0 / 8192.0)
            h_ref[im, lane(k2)] = value[1] * (2.0 / 8192.0)


def spectrum_product(p_ref, h_ref, tw_ref, g_ref):
    @pl.loop(0, 512 // ROWS)
    def _(i):
        re = pl.ds(pl.multiple_of(i * ROWS, ROWS), ROWS)
        im = pl.ds(pl.multiple_of(512 + i * ROWS, ROWS), ROWS)
        points = load_points(p_ref, re, im)
        for b in range(1, 8):
            points[b] = cmul(points[b], (tw_ref[re, lane(b)], tw_ref[im, lane(b)]))
        spec = dft8(points, 1)
        spec = [cmul(v, (h_ref[re, lane(k)], h_ref[im, lane(k)])) for k, v in enumerate(spec)]
        back = dft8(spec, -1)
        for b in range(8):
            value = back[b]
            if b > 0:
                value = cmul_conj(value, (tw_ref[re, lane(b)], tw_ref[im, lane(b)]))
            g_ref[re, lane(b)] = value[0].astype(jnp.bfloat16)
            g_ref[im, lane(b)] = value[1].astype(jnp.bfloat16)


def conv_kernel(sig_ref, filt_ref, skip_ref, table_ref, back_ref, step_ref, out_ref, high, low, p, h, tw, g):
    filter_spectrum(filt_ref, table_ref, step_ref, high, low, p, h, tw)
    stage_matmul(p, table_ref, [sig_ref])
    spectrum_product(p, h, tw, g)
    stage_matmul(p.at[0:512], back_ref, [g])
    for b in range(8):
        out_ref[:, lane(b)] = (
            p[0:512, lane(b)] + skip_ref[...] * sig_ref[:, lane(b)].astype(jnp.float32)
        ).astype(jnp.bfloat16)


def long_mix(signal, filt, skip_cols):
    fwd, back, step = dft_tables()
    sig = signal.reshape(512, 8 * LANES)
    out = pl.pallas_call(
        conv_kernel,
        out_shape=jax.ShapeDtypeStruct((512, 8 * LANES), jnp.bfloat16),
        in_specs=[pl.BlockSpec(memory_space=pltpu.VMEM)] * 6,
        out_specs=pl.BlockSpec(memory_space=pltpu.VMEM),
        scratch_shapes=[
            pltpu.VMEM((512, 1024), jnp.bfloat16),
            pltpu.VMEM((512, 1024), jnp.bfloat16),
            pltpu.VMEM((1024, 1024), jnp.float32),
            pltpu.VMEM((1024, 1024), jnp.float32),
            pltpu.VMEM((1024, 1024), jnp.float32),
            pltpu.VMEM((1024, 1024), jnp.bfloat16),
        ],
        compiler_params=pltpu.CompilerParams(vmem_limit_bytes=56 << 20),
    )(sig, filt, skip_cols[None, :], jnp.asarray(fwd), jnp.asarray(back), jnp.asarray(step))
    return out.reshape(signal.shape)


def short_filter(stream, rim_rows, taps_mine, stream_index, seg_count):
    token_rows, model_channel_width = stream.shape
    seg_len = token_rows // seg_count
    extended = jnp.concatenate([rim_rows, stream], 0)
    summed = jnp.zeros((seg_count, seg_len, model_channel_width), jnp.float32)
    for offset in range(3):
        shifted = extended[2 - offset : 2 - offset + token_rows].reshape(
            seg_count, seg_len, model_channel_width
        )
        summed = summed + shifted.astype(jnp.float32) * taps_mine[:, offset, stream_index, :][
            :, None, :
        ].astype(jnp.float32)
    return summed


def local(
    q_stream,
    k_stream,
    v_stream,
    lang_ids,
    short_taps,
    adapter_down,
    adapter_up,
    long_filter,
    bypass_coefficient,
):
    q_rows, k_rows, v_rows = (q_stream[0], k_stream[0], v_stream[0])
    token_rows, model_channel_width = q_rows.shape
    seg_count = lang_ids.shape[1]
    my_langs = lang_ids[0]
    lang_dev = short_taps.shape[0]
    groups = lax.axis_size("lang")
    wanted = lax.all_gather(my_langs, "lang", axis=0, tiled=True)
    local_ids = wanted - lax.axis_index("lang") * lang_dev
    table = (local_ids[:, None] == jnp.arange(lang_dev, dtype=jnp.int32)[None, :]).astype(
        jnp.bfloat16
    )
    send_down = jnp.einsum(
        "sl,lrd->srd", table, adapter_down, preferred_element_type=jnp.float32
    ).astype(jnp.bfloat16)
    send_up = jnp.einsum(
        "sl,lrd->srd", table, adapter_up, preferred_element_type=jnp.float32
    ).astype(jnp.bfloat16)
    send_taps = jnp.einsum(
        "sl,ljkd->sjkd", table, short_taps, preferred_element_type=jnp.float32
    ).astype(jnp.bfloat16)
    got_down, got_up, got_taps = (
        lax.all_to_all(
            send_down.reshape((groups, seg_count) + send_down.shape[1:]),
            "lang",
            split_axis=0,
            concat_axis=0,
            tiled=True,
        ),
        lax.all_to_all(
            send_up.reshape((groups, seg_count) + send_up.shape[1:]),
            "lang",
            split_axis=0,
            concat_axis=0,
            tiled=True,
        ),
        lax.all_to_all(
            send_taps.reshape((groups, seg_count) + send_taps.shape[1:]),
            "lang",
            split_axis=0,
            concat_axis=0,
            tiled=True,
        ),
    )
    down_mine = jnp.sum(got_down.astype(jnp.float32), axis=0).astype(jnp.bfloat16)
    up_mine = jnp.sum(got_up.astype(jnp.float32), axis=0).astype(jnp.bfloat16)
    taps_mine = jnp.sum(got_taps.astype(jnp.float32), axis=0).astype(jnp.bfloat16)
    rims = shifted_2(jnp.stack([q_rows[-2:], k_rows[-2:], v_rows[-2:]]), "seq", 1)
    qshort = short_filter(q_rows, rims[0], taps_mine, 0, seg_count).astype(jnp.bfloat16)
    query_local_smoothed = short_filter(k_rows, rims[1], taps_mine, 1, seg_count)
    payload_local_smoothed = short_filter(v_rows, rims[2], taps_mine, 2, seg_count)
    modulating_cosine = (
        (query_local_smoothed * payload_local_smoothed)
        .astype(jnp.bfloat16)
        .reshape(token_rows, model_channel_width)
    )
    low = jnp.einsum("snd,srd->snr", qshort, down_mine, preferred_element_type=jnp.float32).astype(
        jnp.bfloat16
    )
    gate = qshort.astype(jnp.float32) + jnp.einsum(
        "snr,srd->snd", low, up_mine, preferred_element_type=jnp.float32
    )
    gate = gate.reshape(token_rows, model_channel_width)
    seq_devs = lax.axis_size("seq")
    per_seq = model_channel_width // seq_devs
    seq_place = lax.axis_index("seq")
    feature_indices = lax.all_to_all(
        modulating_cosine, "seq", split_axis=1, concat_axis=0, tiled=True
    )
    skip_cols = lax.dynamic_slice_in_dim(bypass_coefficient, seq_place * per_seq, per_seq, 0)
    gated_combination = long_mix(feature_indices, long_filter, skip_cols)
    back = lax.all_to_all(gated_combination, "seq", split_axis=0, concat_axis=1, tiled=True)
    return (gate * back.astype(jnp.float32)).astype(jnp.bfloat16)[None]


def solution(mesh):
    placed = (
        P("lang", "seq", None),
        P("lang", "seq", None),
        P("lang", "seq", None),
        P("lang", "seq"),
        P("lang", None, None, None),
        P("lang", None, None),
        P("lang", None, None),
        P(None, "seq"),
        P(),
    )
    return jax.shard_map(
        local, mesh=mesh, in_specs=placed, out_specs=P("lang", "seq", None), check_vma=False
    )
```

```python
import math

import jax
import jax.numpy as jnp
import ml_dtypes
import numpy as np
from jax import lax
from jax.experimental import pallas as pl
from jax.experimental.pallas import tpu as pltpu
from jax.sharding import PartitionSpec as P

LANES = 128
ROWS = 16


def dft_tables():
    k1 = np.arange(512)[:, None]
    a = np.arange(512)[None, :]
    ang = 2.0 * np.pi * ((2 * k1 + 1) * a % 2048) / 2048.0
    table = np.concatenate([np.cos(ang), -np.sin(ang)], 0).astype(np.float32)
    one = 2.0 * np.pi * (2 * np.arange(512) + 1) / 16384.0
    step = np.stack([np.cos(one), -np.sin(one)]).astype(np.float32)
    step = np.ascontiguousarray(np.broadcast_to(step[:, :, None], (2, 512, LANES)))
    fwd = table.astype(ml_dtypes.bfloat16)
    return fwd, np.ascontiguousarray(fwd.T), step


def cadd(p, q):
    return p[0] + q[0], p[1] + q[1]


def csub(p, q):
    return p[0] - q[0], p[1] - q[1]


def cmul(p, q):
    return p[0] * q[0] - p[1] * q[1], p[0] * q[1] + p[1] * q[0]


def cmul_conj(p, q):
    return p[0] * q[0] + p[1] * q[1], p[1] * q[0] - p[0] * q[1]


def quarter(p, sign):
    return (p[1], -p[0]) if sign > 0 else (-p[1], p[0])


def dft4(z0, z1, z2, z3, sign):
    s0, s1 = cadd(z0, z2), csub(z0, z2)
    s2, s3 = cadd(z1, z3), quarter(csub(z1, z3), sign)
    return cadd(s0, s2), cadd(s1, s3), csub(s0, s2), csub(s1, s3)


def dft8(z, sign):
    half = math.sqrt(0.5)
    even = dft4(z[0], z[2], z[4], z[6], sign)
    odd = dft4(z[1], z[3], z[5], z[7], sign)
    o1, o3 = odd[1], odd[3]
    if sign > 0:
        o1 = ((o1[0] + o1[1]) * half, (o1[1] - o1[0]) * half)
        o3 = ((o3[1] - o3[0]) * half, (o3[0] + o3[1]) * -half)
    else:
        o1 = ((o1[0] - o1[1]) * half, (o1[0] + o1[1]) * half)
        o3 = ((o3[0] + o3[1]) * -half, (o3[0] - o3[1]) * half)
    turned = (odd[0], o1, quarter(odd[2], sign), o3)
    return [cadd(e, o) for e, o in zip(even, turned)] + [csub(e, o) for e, o in zip(even, turned)]


def lane(b):
    return slice(b * LANES, (b + 1) * LANES)


def stage_matmul(out_ref, left_ref, right_refs, width=256):
    columns = out_ref.shape[1]

    @pl.loop(0, columns // width)
    def _(j):
        cols = pl.ds(pl.multiple_of(j * width, width), width)
        total = None
        for right_ref in right_refs:
            term = jnp.dot(left_ref[...], right_ref[:, cols], preferred_element_type=jnp.float32)
            total = term if total is None else total + term
        out_ref[:, cols] = total


def load_points(p_ref, rows_re, rows_im):
    return [(p_ref[rows_re, lane(b)], p_ref[rows_im, lane(b)]) for b in range(8)]


def filter_spectrum(filt_ref, table_ref, step_ref, high_ref, low_ref, p_ref, h_ref, tw_ref):
    for b in range(8):
        @pl.loop(0, 4)
        def _(i):
            rows = filt_ref[pl.ds(i * 1024 + b, 128, stride=8), :]
            high = rows.astype(jnp.bfloat16)
            at = pl.ds(pl.multiple_of(i * 128, 128), 128)
            high_ref[at, lane(b)] = high
            low_ref[at, lane(b)] = (rows - high.astype(jnp.float32)).astype(jnp.bfloat16)
    stage_matmul(p_ref, table_ref, [high_ref, low_ref])

    @pl.loop(0, 512 // ROWS)
    def _(i):
        re = pl.ds(pl.multiple_of(i * ROWS, ROWS), ROWS)
        im = pl.ds(pl.multiple_of(512 + i * ROWS, ROWS), ROWS)
        points = load_points(p_ref, re, im)
        step = (step_ref[0, re, :], step_ref[1, re, :])
        turn = step
        for b in range(1, 8):
            tw_ref[re, lane(b)] = turn[0]
            tw_ref[im, lane(b)] = turn[1]
            points[b] = cmul(points[b], turn)
            if b < 7:
                turn = cmul(turn, step)
        for k2, value in enumerate(dft8(points, 1)):
            h_ref[re, lane(k2)] = value[0] * (2.0 / 8192.0)
            h_ref[im, lane(k2)] = value[1] * (2.0 / 8192.0)


def spectrum_product(p_ref, h_ref, tw_ref, g_ref):
    @pl.loop(0, 512 // ROWS)
    def _(i):
        re = pl.ds(pl.multiple_of(i * ROWS, ROWS), ROWS)
        im = pl.ds(pl.multiple_of(512 + i * ROWS, ROWS), ROWS)
        points = load_points(p_ref, re, im)
        for b in range(1, 8):
            points[b] = cmul(points[b], (tw_ref[re, lane(b)], tw_ref[im, lane(b)]))
        spec = dft8(points, 1)
        spec = [cmul(v, (h_ref[re, lane(k)], h_ref[im, lane(k)])) for k, v in enumerate(spec)]
        back = dft8(spec, -1)
        for b in range(8):
            value = back[b]
            if b > 0:
                value = cmul_conj(value, (tw_ref[re, lane(b)], tw_ref[im, lane(b)]))
            g_ref[re, lane(b)] = value[0].astype(jnp.bfloat16)
            g_ref[im, lane(b)] = value[1].astype(jnp.bfloat16)


MESH = pl.DeviceIdType.MESH
PEERS = 3


def pick_tables():
    pick = np.zeros((160, 128), np.float32)
    back = np.zeros((128, 128), np.float32)
    for b in range(-2, 8):
        for a in range(16):
            t = 8 * a + b
            if t >= 0:
                pick[(b + 2) * 16 + a, t] = 1.0
                if b >= 0:
                    back[t, b * 16 + a] = 1.0
    return pick.astype(ml_dtypes.bfloat16), back.astype(ml_dtypes.bfloat16)


class Gather:
    def __init__(self, buf, per, sems, y, me):
        self.buf, self.per, self.sems, self.y, self.me = buf, per, sems, y, me

    def part(self, owner):
        return self.buf.at[pl.ds((owner * 2 + lax.rem(self.me, 2)) * self.per, self.per)]

    def across(self, r):
        mine = self.part(self.y)
        return pltpu.make_async_remote_copy(
            src_ref=mine, dst_ref=mine, send_sem=self.sems.at[0, r - 1], recv_sem=self.sems.at[1, r - 1],
            device_id={"lang": lax.rem(self.y + r, 4)}, device_id_type=MESH,
        )

    def beside(self, r):
        theirs = self.part(lax.rem(self.y + 4 - r, 4))
        return pltpu.make_async_remote_copy(
            src_ref=theirs, dst_ref=theirs, send_sem=self.sems.at[2, r - 1], recv_sem=self.sems.at[3, r - 1],
            device_id={"seq": self.me + 1 - 2 * lax.rem(self.me, 2)}, device_id_type=MESH,
        )

    def start(self):
        for r in (2, 1, 3):
            self.across(r).start()

    def sent(self):
        for r in (2, 1, 3):
            self.across(r).wait_send()

    def forward(self):
        for r in (1, 3, 2):
            self.across(r).wait_recv()
            self.beside(r).start()

    def finish(self):
        for r in (1, 3, 2):
            self.beside(r).wait_recv()
        for r in (1, 3, 2):
            self.beside(r).wait_send()


def columns(d, width=LANES):
    return pl.ds(pl.multiple_of(d * width, width), width)


def tap_rows(sel_ref, rows, cols):
    return jnp.concatenate(
        [jnp.broadcast_to(sel_ref[s, pl.ds(rows[s], 1), cols], (8, LANES)) for s in range(2)], 0
    )


def short_block(pos_ref, taps, b, cols):
    total = None
    for j in range(3):
        term = pos_ref[pl.ds((b + 2 - j) * 16, 16), cols] * taps[j]
        total = term if total is None else total + term
    return total


def fused_kernel(
    lang_ref, skip_ref, pick_ref, unpick_ref, q_in, k_in, v_in, taps_in, down_in, up_in, filt_in, table_in,
    back_in, step_in, out_ref,
    qv, kv, vv, qp, kp, vp, traw, t32, tq32, taps_kv, taps_q, tsel, tqsel, down_all, up_all, down2, up2,
    halo32, halo_out, halo_in, send_x, recv_x, filt, table, back, step, high, low, p, h, tw, g, send_y, recv_y,
    qs, gate, prod, out, local_sem, halo_sem, kv_sem, tq_sem, down_sem, up_sem, x_send, x_recv, y_send, y_recv,
    out_sem,
):
    y = lax.axis_index("lang")
    me = lax.axis_index("seq")
    loads = [
        pltpu.make_async_copy(src, dst, local_sem.at[i])
        for i, (src, dst) in enumerate([
            (taps_in, traw), (k_in.at[0], kv), (v_in.at[0], vv), (q_in.at[0], qv),
            (down_in, down_all.at[pl.ds(4 * y, 4)]), (up_in, up_all.at[pl.ds(4 * y, 4)]),
            (filt_in, filt), (table_in, table), (back_in, back), (step_in, step),
        ])
    ]
    for load in loads:
        load.start()

    barrier = pltpu.get_barrier_semaphore()
    for r in range(1, 4):
        pl.semaphore_signal(barrier, inc=1, device_id={"lang": lax.rem(y + r, 4)}, device_id_type=MESH)

    @pl.loop(1, 32)
    def _(r):
        pl.semaphore_signal(barrier, inc=1, device_id={"seq": lax.rem(me + r, 32)}, device_id_type=MESH)

    kv_get = Gather(taps_kv, 2, kv_sem, y, me)
    tq_get = Gather(taps_q, 1, tq_sem, y, me)
    down_get = Gather(down_all, 2, down_sem, y, me)
    up_get = Gather(up_all, 2, up_sem, y, me)

    t32[...] = jnp.zeros_like(t32)
    tq32[...] = jnp.zeros_like(tq32)
    loads[0].wait()
    for l in range(4):
        for j in range(3):
            three = traw[l, j].astype(jnp.float32)
            t32[l, pl.ds(2 * j, 2), :] = three[1:3]
            tq32[l // 2, pl.ds((l % 2) * 4 + j, 1), :] = three[0:1]
    taps_kv[pl.ds(4 * y, 4)] = t32[...].astype(jnp.bfloat16)
    taps_q[pl.ds(2 * y, 2)] = tq32[...].astype(jnp.bfloat16)
    pl.semaphore_wait(barrier, 34)
    kv_get.start()

    halo32[...] = jnp.zeros_like(halo32)
    for s, (load, raw, pos) in enumerate([(loads[1], kv, kp), (loads[2], vv, vp), (loads[3], qv, qp)]):
        load.wait()

        @pl.loop(0, 8)
        def _(i, raw=raw, pos=pos):
            cols = columns(i, 512)
            pos[:, cols] = jnp.dot(pick_ref[...], raw[:, cols], preferred_element_type=jnp.float32)

        halo32[pl.ds(2 * s, 1), :] = pos[pl.ds(143, 1), :]
        halo32[pl.ds(2 * s + 1, 1), :] = pos[pl.ds(159, 1), :]
    halo_out[...] = halo32[...].astype(jnp.bfloat16)
    halo = pltpu.make_async_remote_copy(
        src_ref=halo_out, dst_ref=halo_in, send_sem=halo_sem.at[0], recv_sem=halo_sem.at[1],
        device_id={"seq": lax.rem(me + 1, 32)}, device_id_type=MESH,
    )
    halo.start()

    kv_get.forward()
    tq_get.start()
    loads[4].wait()
    loads[5].wait()
    down_get.start()
    up_get.start()
    halo.wait_recv()
    halo32[...] = jnp.where(me > 0, halo_in[...].astype(jnp.float32), 0.0)
    for s, pos in enumerate([kp, vp, qp]):
        pos[pl.ds(0, 1), :] = halo32[pl.ds(2 * s, 1), :]
        pos[pl.ds(16, 1), :] = halo32[pl.ds(2 * s + 1, 1), :]
    kv_get.finish()
    langs = [lang_ref[0, s] for s in range(2)]
    for s in range(2):
        tsel[s] = taps_kv[langs[s]].astype(jnp.float32)

    def carrier(d, put):
        cols = columns(d)
        taps = [[tap_rows(tsel, (2 * j + n,) * 2, cols) for j in range(3)] for n in range(2)]
        for b in range(8):
            put(b, (short_block(kp, taps[0], b, cols) * short_block(vp, taps[1], b, cols)).astype(jnp.bfloat16))

    def x_copy(r):
        return pltpu.make_async_remote_copy(
            src_ref=send_x.at[r], dst_ref=recv_x.at[pl.ds(pl.multiple_of(me * 16, 16), 16), :],
            send_sem=x_send.at[r], recv_sem=x_recv.at[r],
            device_id={"seq": lax.bitwise_xor(me, r)}, device_id_type=MESH,
        )

    @pl.loop(1, 32)
    def _(r):
        def put(b, value):
            send_x[r, :, lane(b)] = value

        carrier(lax.bitwise_xor(me, r), put)
        x_copy(r).start()

    own = pl.ds(pl.multiple_of(me * 16, 16), 16)

    def put_own(b, value):
        recv_x[own, lane(b)] = value

    carrier(me, put_own)

    for load in loads[6:]:
        load.wait()
    filter_spectrum(filt, table, step, high, low, p, h, tw)

    @pl.loop(1, 32)
    def _(r):
        x_copy(r).wait_recv()

    stage_matmul(p, table, [recv_x])
    spectrum_product(p, h, tw, g)
    skip = skip_ref[pl.ds(me, 1), :]

    def y_copy(r):
        d = lax.bitwise_xor(me, r)
        return pltpu.make_async_remote_copy(
            src_ref=send_y.at[pl.ds(pl.multiple_of(d * 16, 16), 16), :], dst_ref=recv_y.at[me],
            send_sem=y_send.at[r], recv_sem=y_recv.at[r],
            device_id={"seq": d}, device_id_type=MESH,
        )

    for half in range(2):
        first = lax.bitwise_xor(lax.div(me, 16), half) * 256
        rows = pl.ds(pl.multiple_of(first, 256), 256)

        @pl.loop(0, 4)
        def _(i):
            cols = columns(i, 256)
            conv = jnp.dot(back[rows, :], g[:, cols], preferred_element_type=jnp.float32)
            both = jnp.concatenate([skip, skip], 1)
            send_y[rows, cols] = (conv + both * recv_x[rows, cols].astype(jnp.float32)).astype(jnp.bfloat16)

        @pl.loop(max(1, 16 * half), 16 * half + 16)
        def _(r):
            y_copy(r).start()

    tq_get.forward()
    down_get.forward()
    up_get.forward()
    tq_get.finish()
    for s in range(2):
        pair = taps_q[lax.div(langs[s], 2)].astype(jnp.float32)
        tqsel[s, 0:4, :] = jnp.where(lax.rem(langs[s], 2) > 0, pair[4:8], pair[0:4])

    @pl.loop(0, 32)
    def _(d):
        cols = columns(d)
        taps = [tap_rows(tqsel, (j, j), cols) for j in range(3)]
        for b in range(8):
            qs[pl.ds(b * 16, 16), cols] = short_block(qp, taps, b, cols).astype(jnp.bfloat16)

    down_get.finish()
    up_get.finish()
    for s in range(2):
        down2[pl.ds(16 * s, 16), :] = down_all[langs[s]]
        up2[pl.ds(16 * s, 16), :] = up_all[langs[s]]
    lows = lax.dot_general(
        qs[...], down2[...], (((1,), (1,)), ((), ())), preferred_element_type=jnp.float32
    )
    row_seg = lax.rem(lax.div(lax.broadcasted_iota(jnp.int32, (128, 32), 0), 8), 2)
    col_seg = lax.div(lax.broadcasted_iota(jnp.int32, (128, 32), 1), 16)
    lows = jnp.where(row_seg == col_seg, lows, 0.0).astype(jnp.bfloat16)

    @pl.loop(0, 8)
    def _(i):
        cols = columns(i, 512)
        gate[:, cols] = qs[:, cols].astype(jnp.float32) + jnp.dot(
            lows, up2[:, cols], preferred_element_type=jnp.float32
        )

    recv_y[me] = send_y[own, :]

    def out_copy(i):
        cols = columns(i, 256)
        return pltpu.make_async_copy(out.at[:, cols], out_ref.at[0, :, cols], out_sem.at[i])

    @pl.loop(0, 16)
    def _(i):
        chip = lax.bitwise_xor(lax.div(me, 2), i)
        cols = columns(chip, 256)

        @pl.when(i > 0)
        def _():
            y_copy(2 * i).wait_recv()

        y_copy(2 * i + 1).wait_recv()
        for core in range(2):
            s = 2 * chip + core
            for b in range(8):
                piece = gate[pl.ds(b * 16, 16), columns(s)] * recv_y[s, :, lane(b)].astype(jnp.float32)
                prod[pl.ds(b * 16, 16), lane(core)] = piece.astype(jnp.bfloat16)
        out[:, cols] = jnp.dot(
            unpick_ref[...], prod[...], preferred_element_type=jnp.float32
        ).astype(jnp.bfloat16)
        out_copy(chip).start()

    halo.wait_send()
    for get in (kv_get, tq_get, down_get, up_get):
        get.sent()

    @pl.loop(1, 32)
    def _(r):
        x_copy(r).wait_send()
        y_copy(r).wait_send()

    @pl.loop(0, 16)
    def _(i):
        out_copy(i).wait()


def local(q_stream, k_stream, v_stream, lang_ids, short_taps, adapter_down, adapter_up, long_filter, bypass_coefficient):
    fwd, back, step = dft_tables()
    pick, unpick = pick_tables()
    bf16, f32 = jnp.bfloat16, jnp.float32
    vmem = pl.BlockSpec(memory_space=pltpu.VMEM)
    anywhere = pl.BlockSpec(memory_space=pl.ANY)
    dma = pltpu.SemaphoreType.DMA
    arrays = [
        ((128, 4096), bf16), ((128, 4096), bf16), ((128, 4096), bf16),
        ((160, 4096), f32), ((160, 4096), f32), ((160, 4096), f32),
        ((4, 3, 3, 4096), bf16), ((4, 8, 4096), f32), ((2, 8, 4096), f32),
        ((16, 8, 4096), bf16), ((8, 8, 4096), bf16), ((2, 8, 4096), f32), ((2, 8, 4096), f32),
        ((16, 16, 4096), bf16), ((16, 16, 4096), bf16), ((32, 4096), bf16), ((32, 4096), bf16),
        ((8, 4096), f32), ((8, 4096), bf16), ((8, 4096), bf16),
        ((32, 16, 1024), bf16), ((512, 1024), bf16),
        ((4096, 128), f32), ((1024, 512), bf16), ((512, 1024), bf16), ((2, 512, 128), f32),
        ((512, 1024), bf16), ((512, 1024), bf16),
        ((1024, 1024), f32), ((1024, 1024), f32), ((1024, 1024), f32), ((1024, 1024), bf16),
        ((512, 1024), bf16), ((32, 16, 1024), bf16),
        ((128, 4096), bf16), ((128, 4096), f32), ((128, 256), bf16), ((128, 4096), bf16),
    ]
    return pl.pallas_call(
        fused_kernel,
        out_shape=jax.ShapeDtypeStruct(q_stream.shape, bf16),
        in_specs=[pl.BlockSpec(memory_space=pltpu.SMEM)] + [vmem] * 3 + [anywhere] * 10,
        out_specs=anywhere,
        scratch_shapes=[pltpu.VMEM(shape, kind) for shape, kind in arrays]
        + [dma((10,)), dma((2,)), dma((4, PEERS)), dma((4, PEERS)), dma((4, PEERS)), dma((4, PEERS))]
        + [dma((32,))] * 4
        + [dma((16,))],
        compiler_params=pltpu.CompilerParams(
            collective_id=0, has_side_effects=True, vmem_limit_bytes=60 << 20
        ),
    )(
        lang_ids, bypass_coefficient.reshape(32, 128), jnp.asarray(pick), jnp.asarray(unpick),
        q_stream, k_stream, v_stream, short_taps, adapter_down, adapter_up, long_filter,
        jnp.asarray(fwd), jnp.asarray(back), jnp.asarray(step),
    )


def solution(mesh):
    placed = (
        P("lang", "seq", None),
        P("lang", "seq", None),
        P("lang", "seq", None),
        P("lang", "seq"),
        P("lang", None, None, None),
        P("lang", None, None),
        P("lang", None, None),
        P(None, "seq"),
        P(),
    )
    return jax.shard_map(
        local, mesh=mesh, in_specs=placed, out_specs=P("lang", "seq", None), check_vma=False
    )
```

```python
import math

import jax
import jax.numpy as jnp
import ml_dtypes
import numpy as np
from jax import lax
from jax.experimental import pallas as pl
from jax.experimental.pallas import tpu as pltpu
from jax.sharding import PartitionSpec as P

LANES = 128
ROWS = 16


def dft_tables():
    k1 = np.arange(512)[:, None]
    a = np.arange(512)[None, :]
    ang = 2.0 * np.pi * ((2 * k1 + 1) * a % 2048) / 2048.0
    table = np.concatenate([np.cos(ang), -np.sin(ang)], 0).astype(np.float32)
    one = 2.0 * np.pi * (2 * np.arange(512) + 1) / 16384.0
    step = np.stack([np.cos(one), -np.sin(one)]).astype(np.float32)
    step = np.ascontiguousarray(np.broadcast_to(step[:, :, None], (2, 512, LANES)))
    fwd = table.astype(ml_dtypes.bfloat16)
    return fwd, np.ascontiguousarray(fwd.T), step


def cadd(p, q):
    return p[0] + q[0], p[1] + q[1]


def csub(p, q):
    return p[0] - q[0], p[1] - q[1]


def cmul(p, q):
    return p[0] * q[0] - p[1] * q[1], p[0] * q[1] + p[1] * q[0]


def cmul_conj(p, q):
    return p[0] * q[0] + p[1] * q[1], p[1] * q[0] - p[0] * q[1]


def quarter(p, sign):
    return (p[1], -p[0]) if sign > 0 else (-p[1], p[0])


def dft4(z0, z1, z2, z3, sign):
    s0, s1 = cadd(z0, z2), csub(z0, z2)
    s2, s3 = cadd(z1, z3), quarter(csub(z1, z3), sign)
    return cadd(s0, s2), cadd(s1, s3), csub(s0, s2), csub(s1, s3)


def dft8(z, sign):
    half = math.sqrt(0.5)
    even = dft4(z[0], z[2], z[4], z[6], sign)
    odd = dft4(z[1], z[3], z[5], z[7], sign)
    o1, o3 = odd[1], odd[3]
    if sign > 0:
        o1 = ((o1[0] + o1[1]) * half, (o1[1] - o1[0]) * half)
        o3 = ((o3[1] - o3[0]) * half, (o3[0] + o3[1]) * -half)
    else:
        o1 = ((o1[0] - o1[1]) * half, (o1[0] + o1[1]) * half)
        o3 = ((o3[0] + o3[1]) * -half, (o3[0] - o3[1]) * half)
    turned = (odd[0], o1, quarter(odd[2], sign), o3)
    return [cadd(e, o) for e, o in zip(even, turned)] + [csub(e, o) for e, o in zip(even, turned)]


def lane(b):
    return slice(b * LANES, (b + 1) * LANES)


def stage_matmul(out_ref, left_ref, right_refs, width=256):
    columns = out_ref.shape[1]

    @pl.loop(0, columns // width)
    def _(j):
        cols = pl.ds(pl.multiple_of(j * width, width), width)
        total = None
        for right_ref in right_refs:
            term = jnp.dot(left_ref[...], right_ref[:, cols], preferred_element_type=jnp.float32)
            total = term if total is None else total + term
        out_ref[:, cols] = total


def load_points(p_ref, rows_re, rows_im):
    return [(p_ref[rows_re, lane(b)], p_ref[rows_im, lane(b)]) for b in range(8)]


def filter_spectrum(filt_ref, table_ref, step_ref, high_ref, low_ref, p_ref, h_ref, tw_ref):
    for b in range(8):
        @pl.loop(0, 4)
        def _(i):
            rows = filt_ref[pl.ds(i * 1024 + b, 128, stride=8), :]
            high = rows.astype(jnp.bfloat16)
            at = pl.ds(pl.multiple_of(i * 128, 128), 128)
            high_ref[at, lane(b)] = high
            low_ref[at, lane(b)] = (rows - high.astype(jnp.float32)).astype(jnp.bfloat16)
    stage_matmul(p_ref, table_ref, [high_ref, low_ref])

    @pl.loop(0, 512 // ROWS)
    def _(i):
        re = pl.ds(pl.multiple_of(i * ROWS, ROWS), ROWS)
        im = pl.ds(pl.multiple_of(512 + i * ROWS, ROWS), ROWS)
        points = load_points(p_ref, re, im)
        step = (step_ref[0, re, :], step_ref[1, re, :])
        turn = step
        for b in range(1, 8):
            tw_ref[re, lane(b)] = turn[0]
            tw_ref[im, lane(b)] = turn[1]
            points[b] = cmul(points[b], turn)
            if b < 7:
                turn = cmul(turn, step)
        for k2, value in enumerate(dft8(points, 1)):
            h_ref[re, lane(k2)] = value[0] * (2.0 / 8192.0)
            h_ref[im, lane(k2)] = value[1] * (2.0 / 8192.0)


def spectrum_product(p_ref, h_ref, tw_ref, g_ref):
    @pl.loop(0, 512 // ROWS)
    def _(i):
        re = pl.ds(pl.multiple_of(i * ROWS, ROWS), ROWS)
        im = pl.ds(pl.multiple_of(512 + i * ROWS, ROWS), ROWS)
        points = load_points(p_ref, re, im)
        for b in range(1, 8):
            points[b] = cmul(points[b], (tw_ref[re, lane(b)], tw_ref[im, lane(b)]))
        spec = dft8(points, 1)
        spec = [cmul(v, (h_ref[re, lane(k)], h_ref[im, lane(k)])) for k, v in enumerate(spec)]
        back = dft8(spec, -1)
        for b in range(8):
            value = back[b]
            if b > 0:
                value = cmul_conj(value, (tw_ref[re, lane(b)], tw_ref[im, lane(b)]))
            g_ref[re, lane(b)] = value[0].astype(jnp.bfloat16)
            g_ref[im, lane(b)] = value[1].astype(jnp.bfloat16)


MESH = pl.DeviceIdType.MESH
GROUP = 2


def pick_tables():
    pick = np.zeros((160, 128), np.float32)
    back = np.zeros((128, 128), np.float32)
    for b in range(-2, 8):
        for a in range(16):
            t = 8 * a + b
            if t >= 0:
                pick[(b + 2) * 16 + a, t] = 1.0
                if b >= 0:
                    back[t, b * 16 + a] = 1.0
    return pick.astype(ml_dtypes.bfloat16), back.astype(ml_dtypes.bfloat16)


class Panels:
    def __init__(self, part, sems, y, me):
        self.part, self.sems, self.y, self.me = part, sems, y, me

    def move(self, owner, kind, r, device):
        ref = self.part(owner)
        return pltpu.make_async_remote_copy(
            src_ref=ref, dst_ref=ref, send_sem=self.sems.at[kind, r - 1], recv_sem=self.sems.at[kind + 1, r - 1],
            device_id=device, device_id_type=MESH,
        )

    def across(self, r):
        return self.move(self.y, 0, r, {"lang": lax.rem(self.y + r, 4)})

    def relay(self, r):
        return self.move(lax.rem(self.y + 4 - r, 4), 0, 2, {"lang": lax.rem(self.y + r, 4)})

    def beside(self, r):
        return self.move(lax.rem(self.y + 4 - r, 4), 2, r, {"seq": lax.bitwise_xor(self.me, 1)})


def columns(d, width=LANES):
    return pl.ds(pl.multiple_of(d * width, width), width)


def tap_rows(sel_ref, rows, cols):
    return jnp.concatenate(
        [jnp.broadcast_to(sel_ref[s, pl.ds(rows[s], 1), cols], (8, LANES)) for s in range(2)], 0
    )


def short_block(pos_ref, taps, b, cols):
    total = None
    for j in range(3):
        term = pos_ref[pl.ds((b + 2 - j) * 16, 16), cols] * taps[j]
        total = term if total is None else total + term
    return total


def fused_kernel(
    lang_ref, skip_ref, pick_ref, unpick_ref, q_in, k_in, v_in, taps_in, down_in, up_in, filt_in, table_in,
    back_in, step_in, out_ref,
    qv, kv, vv, qp, kp, vp, traw, tk_0, tk_1, tk_2, tk_3, tq_all, tsel, tqsel, down_all, up_all, down2, up2,
    halo32, halo_out, halo_in, send_x, recv_x, filt, table, back, step, high, low, p, h, tw, g, send_y, recv_y,
    qs, gate, prod, out, local_sem, halo_sem, tk_sem, tq_sem, down_sem, up_sem, x_send, x_recv, y_send, y_recv,
    out_sem, line_sem, all_sem,
):
    y = lax.axis_index("lang")
    me = lax.axis_index("seq")
    core = lax.rem(me, 2)
    tk_all = [tk_0, tk_1, tk_2, tk_3]
    loads = [
        pltpu.make_async_copy(src, dst, local_sem.at[i])
        for i, (src, dst) in enumerate([
            (taps_in, traw), (k_in.at[0], kv), (v_in.at[0], vv), (q_in.at[0], qv),
            (down_in, down_all.at[pl.ds(4 * y, 4)]), (up_in, up_all.at[pl.ds(4 * y, 4)]),
            (filt_in, filt), (table_in, table), (back_in, back), (step_in, step),
        ])
    ]
    for load in loads:
        load.start()

    barrier = pltpu.get_barrier_semaphore()
    for r in range(1, 4):
        pl.semaphore_signal(barrier, inc=1, device_id={"lang": lax.rem(y + r, 4)}, device_id_type=MESH)
    for r in (1, 2, 4, 6, 8, 16, 24):
        pl.semaphore_signal(barrier, inc=1, device_id={"seq": lax.bitwise_xor(me, r)}, device_id_type=MESH)
    pl.semaphore_signal(barrier, inc=1, device_id={"seq": lax.rem(me + 31, 32)}, device_id_type=MESH)

    def chip_of(i, j):
        return lax.bitwise_xor(lax.div(me, 2), 4 * j + lax.bitwise_xor(j, i))

    half = pl.ds(pl.multiple_of(core * 512, 512), 512)
    halves = pl.ds(pl.multiple_of(core * 2048, 2048), 2048)
    chunks = [
        Panels(lambda owner, i=i: tk_all[i].at[owner, :, :, half], tk_sem.at[i], y, me) for i in range(4)
    ]
    tq_get = Panels(lambda owner: tq_all.at[owner, :, :, halves], tq_sem, y, me)
    down_get = Panels(lambda owner: down_all.at[pl.ds(4 * owner + 2 * core, 2)], down_sem, y, me)
    up_get = Panels(lambda owner: up_all.at[pl.ds(4 * owner + 2 * core, 2)], up_sem, y, me)

    loads[0].wait()
    for i in range(4):
        for j in range(4):
            cols = columns(chip_of(i, j), 256)
            for t in range(3):
                for n in range(2):
                    tk_all[i][y, 2 * t + n, :, 256 * j:256 * j + 256] = traw[t, n + 1, :, cols]
    for t in range(3):
        tq_all[y, t] = traw[t, 0]

    halo32[...] = jnp.zeros_like(halo32)
    for s, (load, raw, pos) in enumerate([(loads[1], kv, kp), (loads[2], vv, vp), (loads[3], qv, qp)]):
        load.wait()

        @pl.loop(0, 8)
        def _(i, raw=raw, pos=pos):
            cols = columns(i, 512)
            pos[:, cols] = jnp.dot(pick_ref[...], raw[:, cols], preferred_element_type=jnp.float32)

        halo32[pl.ds(2 * s, 1), :] = pos[pl.ds(143, 1), :]
        halo32[pl.ds(2 * s + 1, 1), :] = pos[pl.ds(159, 1), :]
    halo_out[...] = halo32[...].astype(jnp.bfloat16)

    pl.semaphore_wait(barrier, 11)
    for get in chunks:
        for r in (2, 1, 3):
            get.across(r).start()
    halo = pltpu.make_async_remote_copy(
        src_ref=halo_out, dst_ref=halo_in, send_sem=halo_sem.at[0], recv_sem=halo_sem.at[1],
        device_id={"seq": lax.rem(me + 1, 32)}, device_id_type=MESH,
    )
    halo.start()
    for r in (2, 4, 6):
        pl.semaphore_signal(line_sem, inc=1, device_id={"seq": lax.bitwise_xor(me, r)}, device_id_type=MESH)
    pl.semaphore_wait(line_sem, 3)
    pl.semaphore_signal(all_sem, inc=1, device_id={"seq": lax.bitwise_xor(me, 1)}, device_id_type=MESH)

    def hand_on(get):
        for r in (1, 3, 2):
            get.across(r).wait_recv()
            get.beside(r).start()

    hand_on(chunks[0])
    halo.wait_recv()
    halo32[...] = jnp.where(me > 0, halo_in[...].astype(jnp.float32), 0.0)
    for s, pos in enumerate([kp, vp, qp]):
        pos[pl.ds(0, 1), :] = halo32[pl.ds(2 * s, 1), :]
        pos[pl.ds(16, 1), :] = halo32[pl.ds(2 * s + 1, 1), :]
    pl.semaphore_wait(all_sem, 1)

    owners = [lax.div(lang_ref[0, s], 4) for s in range(2)]
    places = [lax.rem(lang_ref[0, s], 4) for s in range(2)]

    def chosen(four, s):
        row = lax.broadcasted_iota(jnp.int32, four.shape, 0)
        return jnp.sum(jnp.where(row == places[s], four.astype(jnp.float32), 0.0), axis=0, keepdims=True)

    def carrier(d, tap_cols, put):
        cols = columns(d)
        taps = [[tap_rows(tsel, (2 * j + n,) * 2, tap_cols) for j in range(3)] for n in range(2)]
        for b in range(8):
            put(b, (short_block(kp, taps[0], b, cols) * short_block(vp, taps[1], b, cols)).astype(jnp.bfloat16))

    def x_copy(r):
        return pltpu.make_async_remote_copy(
            src_ref=send_x.at[r], dst_ref=recv_x.at[pl.ds(pl.multiple_of(me * 16, 16), 16), :],
            send_sem=x_send.at[r], recv_sem=x_recv.at[r],
            device_id={"seq": lax.bitwise_xor(me, r)}, device_id_type=MESH,
        )

    for i in range(4):
        for r in (1, 3, 2):
            chunks[i].beside(r).wait_recv()
        if i < 3:
            hand_on(chunks[i + 1])
        for s in range(2):
            for n in range(6):
                tsel[s, pl.ds(n, 1), 1024 * i:1024 * i + 1024] = chosen(tk_all[i][owners[s], n], s)

        @pl.loop(1 if i == 0 else 0, 8)
        def _(k, i=i):
            j, flip = lax.div(k, 2), lax.rem(k, 2)
            r = 8 * j + 2 * lax.bitwise_xor(j, i) + flip

            def put(b, value):
                send_x[r, :, lane(b)] = value

            carrier(lax.bitwise_xor(me, r), columns(8 * i + 2 * j + lax.bitwise_xor(core, flip)), put)
            x_copy(r).start()

        if i == 2:
            loads[4].wait()
            for get in (tq_get, down_get):
                for r in (2, 1, 3) if get is tq_get else (1, 3):
                    get.across(r).start()

    loads[5].wait()
    for r in (3, 1):
        up_get.across(r).start()
    own = pl.ds(pl.multiple_of(me * 16, 16), 16)

    def put_own(b, value):
        recv_x[own, lane(b)] = value

    carrier(me, columns(core), put_own)

    for load in loads[6:]:
        load.wait()
    filter_spectrum(filt, table, step, high, low, p, h, tw)
    down_get.across(1).wait_recv()
    down_get.relay(1).start()
    down_get.beside(1).start()

    @pl.loop(1, 32)
    def _(r):
        x_copy(r).wait_recv()

    stage_matmul(p, table, [recv_x])
    spectrum_product(p, h, tw, g)
    skip = skip_ref[pl.ds(me, 1), :]

    def y_copy(r):
        d = lax.bitwise_xor(me, r)
        j = lax.div(r, 8)
        i = lax.bitwise_xor(lax.rem(lax.div(r, 2), 4), j)
        slot = 8 * i + 2 * j + lax.rem(d, 2)
        return pltpu.make_async_remote_copy(
            src_ref=send_y.at[pl.ds(pl.multiple_of(slot * 16, 16), 16), :], dst_ref=recv_y.at[me],
            send_sem=y_send.at[r], recv_sem=y_recv.at[r],
            device_id={"seq": d}, device_id_type=MESH,
        )

    for i in range(0, 4, GROUP):
        blocks = [
            pl.ds(pl.multiple_of(32 * chip_of(i + n, j), 32), 32) for n in range(GROUP) for j in range(4)
        ]

        @pl.loop(0, 4)
        def _(m, i=i, blocks=blocks):
            cols = columns(m, 256)
            left = jnp.concatenate([back[rows, :] for rows in blocks], 0)
            signal = jnp.concatenate([recv_x[rows, cols] for rows in blocks], 0)
            conv = jnp.dot(left, g[:, cols], preferred_element_type=jnp.float32)
            both = jnp.concatenate([skip, skip], 1)
            send_y[128 * i:128 * (i + GROUP), cols] = (conv + both * signal.astype(jnp.float32)).astype(jnp.bfloat16)

        @pl.loop(8 * i + (1 if i == 0 else 0), 8 * (i + GROUP))
        def _(k):
            n, j, flip = lax.div(k, 8), lax.rem(lax.div(k, 2), 4), lax.rem(k, 2)
            y_copy(8 * j + 2 * lax.bitwise_xor(j, n) + flip).start()

    up_get.across(3).wait_recv()
    up_get.relay(3).start()
    up_get.beside(3).start()
    for r in (1, 3, 2):
        tq_get.across(r).wait_recv()
        tq_get.beside(r).start()
    down_get.across(3).wait_recv()
    down_get.beside(3).start()
    up_get.across(1).wait_recv()
    up_get.beside(1).start()
    for r in (1, 3, 2):
        tq_get.beside(r).wait_recv()
    for s in range(2):
        for t in range(3):
            tqsel[s, pl.ds(t, 1), :] = chosen(tq_all[owners[s], t], s)

    @pl.loop(0, 32)
    def _(d):
        cols = columns(d)
        taps = [tap_rows(tqsel, (j, j), cols) for j in range(3)]
        for b in range(8):
            qs[pl.ds(b * 16, 16), cols] = short_block(qp, taps, b, cols).astype(jnp.bfloat16)

    for get in (down_get, up_get):
        get.across(2).wait_recv()
        get.beside(2).start()
    for get in (down_get, up_get):
        for r in (1, 3, 2):
            get.beside(r).wait_recv()
    for s in range(2):
        down2[pl.ds(16 * s, 16), :] = down_all[lang_ref[0, s]]
        up2[pl.ds(16 * s, 16), :] = up_all[lang_ref[0, s]]
    lows = lax.dot_general(
        qs[...], down2[...], (((1,), (1,)), ((), ())), preferred_element_type=jnp.float32
    )
    row_seg = lax.rem(lax.div(lax.broadcasted_iota(jnp.int32, (128, 32), 0), 8), 2)
    col_seg = lax.div(lax.broadcasted_iota(jnp.int32, (128, 32), 1), 16)
    lows = jnp.where(row_seg == col_seg, lows, 0.0).astype(jnp.bfloat16)

    @pl.loop(0, 8)
    def _(i):
        cols = columns(i, 512)
        gate[:, cols] = qs[:, cols].astype(jnp.float32) + jnp.dot(
            lows, up2[:, cols], preferred_element_type=jnp.float32
        )

    recv_y[me] = send_y[pl.ds(pl.multiple_of(core * 16, 16), 16), :]

    def out_copy(i):
        cols = columns(i, 256)
        return pltpu.make_async_copy(out.at[:, cols], out_ref.at[0, :, cols], out_sem.at[i])

    @pl.loop(0, 16)
    def _(k):
        n, j = lax.div(k, 4), lax.rem(k, 4)
        r = 8 * j + 2 * lax.bitwise_xor(j, n)
        chip = lax.bitwise_xor(lax.div(me, 2), lax.div(r, 2))
        cols = columns(chip, 256)

        @pl.when(k > 0)
        def _():
            y_copy(r).wait_recv()

        y_copy(r + 1).wait_recv()
        for one in range(2):
            s = 2 * chip + one
            for b in range(8):
                piece = gate[pl.ds(b * 16, 16), columns(s)] * recv_y[s, :, lane(b)].astype(jnp.float32)
                prod[pl.ds(b * 16, 16), lane(one)] = piece.astype(jnp.bfloat16)
        out[:, cols] = jnp.dot(
            unpick_ref[...], prod[...], preferred_element_type=jnp.float32
        ).astype(jnp.bfloat16)
        out_copy(chip).start()

    halo.wait_send()
    for get in chunks + [tq_get]:
        for r in (1, 2, 3):
            get.across(r).wait_send()
            get.beside(r).wait_send()
    for get, way in ((down_get, 1), (up_get, 3)):
        for r in (1, 3):
            get.across(r).wait_send()
        get.relay(way).wait_send()
        for r in (1, 2, 3):
            get.beside(r).wait_send()

    @pl.loop(1, 32)
    def _(r):
        x_copy(r).wait_send()
        y_copy(r).wait_send()

    @pl.loop(0, 16)
    def _(i):
        out_copy(i).wait()


def local(q_stream, k_stream, v_stream, lang_ids, short_taps, adapter_down, adapter_up, long_filter, bypass_coefficient):
    fwd, back, step = dft_tables()
    pick, unpick = pick_tables()
    bf16, f32 = jnp.bfloat16, jnp.float32
    vmem = pl.BlockSpec(memory_space=pltpu.VMEM)
    anywhere = pl.BlockSpec(memory_space=pl.ANY)
    dma = pltpu.SemaphoreType.DMA
    arrays = [
        ((128, 4096), bf16), ((128, 4096), bf16), ((128, 4096), bf16),
        ((160, 4096), f32), ((160, 4096), f32), ((160, 4096), f32),
        ((3, 3, 4, 4096), bf16), ] + [((4, 6, 4, 1024), bf16)] * 4 + [((4, 3, 4, 4096), bf16),
        ((2, 8, 4096), f32), ((2, 8, 4096), f32),
        ((16, 16, 4096), bf16), ((16, 16, 4096), bf16), ((32, 4096), bf16), ((32, 4096), bf16),
        ((8, 4096), f32), ((8, 4096), bf16), ((8, 4096), bf16),
        ((32, 16, 1024), bf16), ((512, 1024), bf16),
        ((4096, 128), f32), ((1024, 512), bf16), ((512, 1024), bf16), ((2, 512, 128), f32),
        ((512, 1024), bf16), ((512, 1024), bf16),
        ((1024, 1024), f32), ((1024, 1024), f32), ((1024, 1024), f32), ((1024, 1024), bf16),
        ((512, 1024), bf16), ((32, 16, 1024), bf16),
        ((128, 4096), bf16), ((128, 4096), f32), ((128, 256), bf16), ((128, 4096), bf16),
    ]
    return pl.pallas_call(
        fused_kernel,
        out_shape=jax.ShapeDtypeStruct(q_stream.shape, bf16),
        in_specs=[pl.BlockSpec(memory_space=pltpu.SMEM)] + [vmem] * 3 + [anywhere] * 10,
        out_specs=anywhere,
        scratch_shapes=[pltpu.VMEM(shape, kind) for shape, kind in arrays]
        + [dma((10,)), dma((2,)), dma((4, 4, 3)), dma((4, 3)), dma((4, 3)), dma((4, 3))]
        + [dma((32,))] * 4
        + [dma((16,)), pltpu.SemaphoreType.REGULAR, pltpu.SemaphoreType.REGULAR],
        compiler_params=pltpu.CompilerParams(
            collective_id=0, has_side_effects=True, vmem_limit_bytes=60 << 20
        ),
    )(
        lang_ids, bypass_coefficient.reshape(32, 128), jnp.asarray(pick), jnp.asarray(unpick),
        q_stream, k_stream, v_stream, short_taps.transpose(1, 2, 0, 3), adapter_down, adapter_up, long_filter,
        jnp.asarray(fwd), jnp.asarray(back), jnp.asarray(step),
    )


def solution(mesh):
    placed = (
        P("lang", "seq", None),
        P("lang", "seq", None),
        P("lang", "seq", None),
        P("lang", "seq"),
        P("lang", None, None, None),
        P("lang", None, None),
        P("lang", None, None),
        P(None, "seq"),
        P(),
    )
    return jax.shard_map(
        local, mesh=mesh, in_specs=placed, out_specs=P("lang", "seq", None), check_vma=False
    )
```

```python
import math

import jax
import jax.numpy as jnp
import ml_dtypes
import numpy as np
from jax import lax
from jax.experimental import pallas as pl
from jax.experimental.pallas import tpu as pltpu
from jax.sharding import PartitionSpec as P

LANES = 128
ROWS = 16


def dft_tables():
    k1 = np.arange(512)[:, None]
    a = np.arange(512)[None, :]
    ang = 2.0 * np.pi * ((2 * k1 + 1) * a % 2048) / 2048.0
    table = np.concatenate([np.cos(ang), -np.sin(ang)], 0).astype(np.float32)
    one = 2.0 * np.pi * (2 * np.arange(512) + 1) / 16384.0
    step = np.stack([np.cos(one), -np.sin(one)]).astype(np.float32)
    step = np.ascontiguousarray(np.broadcast_to(step[:, :, None], (2, 512, LANES)))
    fwd = table.astype(ml_dtypes.bfloat16)
    return fwd, np.ascontiguousarray(fwd.T), step


def cadd(p, q):
    return p[0] + q[0], p[1] + q[1]


def csub(p, q):
    return p[0] - q[0], p[1] - q[1]


def cmul(p, q):
    return p[0] * q[0] - p[1] * q[1], p[0] * q[1] + p[1] * q[0]


def cmul_conj(p, q):
    return p[0] * q[0] + p[1] * q[1], p[1] * q[0] - p[0] * q[1]


def quarter(p, sign):
    return (p[1], -p[0]) if sign > 0 else (-p[1], p[0])


def dft4(z0, z1, z2, z3, sign):
    s0, s1 = cadd(z0, z2), csub(z0, z2)
    s2, s3 = cadd(z1, z3), quarter(csub(z1, z3), sign)
    return cadd(s0, s2), cadd(s1, s3), csub(s0, s2), csub(s1, s3)


def dft8(z, sign):
    half = math.sqrt(0.5)
    even = dft4(z[0], z[2], z[4], z[6], sign)
    odd = dft4(z[1], z[3], z[5], z[7], sign)
    o1, o3 = odd[1], odd[3]
    if sign > 0:
        o1 = ((o1[0] + o1[1]) * half, (o1[1] - o1[0]) * half)
        o3 = ((o3[1] - o3[0]) * half, (o3[0] + o3[1]) * -half)
    else:
        o1 = ((o1[0] - o1[1]) * half, (o1[0] + o1[1]) * half)
        o3 = ((o3[0] + o3[1]) * -half, (o3[0] - o3[1]) * half)
    turned = (odd[0], o1, quarter(odd[2], sign), o3)
    return [cadd(e, o) for e, o in zip(even, turned)] + [csub(e, o) for e, o in zip(even, turned)]


def lane(b):
    return slice(b * LANES, (b + 1) * LANES)


def stage_matmul(out_ref, left_ref, right_refs, width=256):
    columns = out_ref.shape[1]

    @pl.loop(0, columns // width)
    def _(j):
        cols = pl.ds(pl.multiple_of(j * width, width), width)
        total = None
        for right_ref in right_refs:
            term = jnp.dot(left_ref[...], right_ref[:, cols], preferred_element_type=jnp.float32)
            total = term if total is None else total + term
        out_ref[:, cols] = total


def load_points(p_ref, rows_re, rows_im):
    return [(p_ref[rows_re, lane(b)], p_ref[rows_im, lane(b)]) for b in range(8)]


def filter_spectrum(filt_ref, table_ref, step_ref, high_ref, low_ref, p_ref, h_ref, tw_ref):
    for b in range(8):
        @pl.loop(0, 4)
        def _(i):
            rows = filt_ref[pl.ds(i * 1024 + b, 128, stride=8), :]
            high = rows.astype(jnp.bfloat16)
            at = pl.ds(pl.multiple_of(i * 128, 128), 128)
            high_ref[at, lane(b)] = high
            low_ref[at, lane(b)] = (rows - high.astype(jnp.float32)).astype(jnp.bfloat16)
    stage_matmul(p_ref, table_ref, [high_ref, low_ref])

    @pl.loop(0, 512 // ROWS)
    def _(i):
        re = pl.ds(pl.multiple_of(i * ROWS, ROWS), ROWS)
        im = pl.ds(pl.multiple_of(512 + i * ROWS, ROWS), ROWS)
        points = load_points(p_ref, re, im)
        step = (step_ref[0, re, :], step_ref[1, re, :])
        turn = step
        for b in range(1, 8):
            tw_ref[re, lane(b)] = turn[0]
            tw_ref[im, lane(b)] = turn[1]
            points[b] = cmul(points[b], turn)
            if b < 7:
                turn = cmul(turn, step)
        for k2, value in enumerate(dft8(points, 1)):
            h_ref[re, lane(k2)] = value[0] * (2.0 / 8192.0)
            h_ref[im, lane(k2)] = value[1] * (2.0 / 8192.0)


def spectrum_product(p_ref, h_ref, tw_ref, g_ref):
    @pl.loop(0, 512 // ROWS)
    def _(i):
        re = pl.ds(pl.multiple_of(i * ROWS, ROWS), ROWS)
        im = pl.ds(pl.multiple_of(512 + i * ROWS, ROWS), ROWS)
        points = load_points(p_ref, re, im)
        for b in range(1, 8):
            points[b] = cmul(points[b], (tw_ref[re, lane(b)], tw_ref[im, lane(b)]))
        spec = dft8(points, 1)
        spec = [cmul(v, (h_ref[re, lane(k)], h_ref[im, lane(k)])) for k, v in enumerate(spec)]
        back = dft8(spec, -1)
        for b in range(8):
            value = back[b]
            if b > 0:
                value = cmul_conj(value, (tw_ref[re, lane(b)], tw_ref[im, lane(b)]))
            g_ref[re, lane(b)] = value[0].astype(jnp.bfloat16)
            g_ref[im, lane(b)] = value[1].astype(jnp.bfloat16)


MESH = pl.DeviceIdType.MESH
GROUP = 2


def pick_tables():
    pick = np.zeros((160, 128), np.float32)
    back = np.zeros((128, 128), np.float32)
    for b in range(-2, 8):
        for a in range(16):
            t = 8 * a + b
            if t >= 0:
                pick[(b + 2) * 16 + a, t] = 1.0
                if b >= 0:
                    back[t, b * 16 + a] = 1.0
    return pick.astype(ml_dtypes.bfloat16), back.astype(ml_dtypes.bfloat16)


class Panels:
    def __init__(self, part, sems, y, me):
        self.part, self.sems, self.y, self.me = part, sems, y, me

    def move(self, owner, kind, r, device):
        ref = self.part(owner)
        return pltpu.make_async_remote_copy(
            src_ref=ref, dst_ref=ref, send_sem=self.sems.at[kind, r - 1], recv_sem=self.sems.at[kind + 1, r - 1],
            device_id=device, device_id_type=MESH,
        )

    def across(self, r):
        return self.move(self.y, 0, r, {"lang": lax.rem(self.y + r, 4)})

    def relay(self, r):
        return self.move(lax.rem(self.y + 4 - r, 4), 0, 2, {"lang": lax.rem(self.y + r, 4)})

    def beside(self, r):
        return self.move(lax.rem(self.y + 4 - r, 4), 2, r, {"seq": lax.bitwise_xor(self.me, 1)})


def columns(d, width=LANES):
    return pl.ds(pl.multiple_of(d * width, width), width)


def tap_rows(sel_ref, rows, cols):
    return jnp.concatenate(
        [jnp.broadcast_to(sel_ref[s, pl.ds(rows[s], 1), cols], (8, LANES)) for s in range(2)], 0
    )


def short_block(pos_ref, taps, b, cols):
    total = None
    for j in range(3):
        term = pos_ref[pl.ds((b + 2 - j) * 16, 16), cols] * taps[j]
        total = term if total is None else total + term
    return total


def fused_kernel(
    lang_ref, skip_ref, pick_ref, unpick_ref, q_in, k_in, v_in, taps_in, down_in, up_in, filt_in, table_in,
    back_in, step_in, out_ref,
    qv, kv, vv, qp, kp, vp, traw, tk_0, tk_1, tk_2, tk_3, tq_all, tsel, tqsel, down_all, up_all, down2, up2,
    halo32, halo_out, halo_in, send_x, recv_x, filt, table, back, step, high, low, p, h, tw, g, send_y, recv_y,
    qs, gate, prod, out, local_sem, halo_sem, tk_sem, tq_sem, down_sem, up_sem, x_send, x_recv, y_send, y_recv,
    out_sem, line_sem, all_sem,
):
    y = lax.axis_index("lang")
    me = lax.axis_index("seq")
    core = lax.rem(me, 2)
    tk_all = [tk_0, tk_1, tk_2, tk_3]
    loads = [
        pltpu.make_async_copy(src, dst, local_sem.at[i])
        for i, (src, dst) in enumerate([
            (taps_in, traw), (k_in.at[0], kv), (v_in.at[0], vv), (q_in.at[0], qv),
            (down_in, down_all.at[pl.ds(4 * y, 4)]), (up_in, up_all.at[pl.ds(4 * y, 4)]),
            (filt_in, filt), (table_in, table), (back_in, back), (step_in, step),
        ])
    ]
    for load in loads:
        load.start()

    barrier = pltpu.get_barrier_semaphore()
    for r in range(1, 4):
        pl.semaphore_signal(barrier, inc=1, device_id={"lang": lax.rem(y + r, 4)}, device_id_type=MESH)
    for r in (1, 2, 4, 6, 8, 16, 24):
        pl.semaphore_signal(barrier, inc=1, device_id={"seq": lax.bitwise_xor(me, r)}, device_id_type=MESH)
    pl.semaphore_signal(barrier, inc=1, device_id={"seq": lax.rem(me + 31, 32)}, device_id_type=MESH)

    def chip_of(i, j):
        return lax.bitwise_xor(lax.div(me, 2), 4 * j + lax.bitwise_xor(j, i))

    halves = pl.ds(pl.multiple_of(core * 2048, 2048), 2048)
    chunks = [
        Panels(lambda owner, i=i: tk_all[i].at[owner], tk_sem.at[i], y, me) for i in range(4)
    ]
    tq_get = Panels(lambda owner: tq_all.at[owner, :, :, halves], tq_sem, y, me)
    down_get = Panels(lambda owner: down_all.at[pl.ds(4 * owner + 2 * core, 2)], down_sem, y, me)
    up_get = Panels(lambda owner: up_all.at[pl.ds(4 * owner + 2 * core, 2)], up_sem, y, me)

    loads[0].wait()
    for i in range(4):
        for j in range(4):
            cols = columns(chip_of(i, j), 256)
            for t in range(3):
                for n in range(2):
                    tk_all[i][y, 2 * t + n, :, 256 * j:256 * j + 256] = traw[t, n + 1, :, cols]
    for t in range(3):
        tq_all[y, t] = traw[t, 0]

    halo32[...] = jnp.zeros_like(halo32)
    for s, (load, raw) in enumerate([(loads[1], kv), (loads[2], vv), (loads[3], qv)]):
        load.wait()
        halo32[pl.ds(2 * s, 2), :] = raw[112:128, :].astype(jnp.float32)[14:16]
    halo_out[...] = halo32[...].astype(jnp.bfloat16)

    pl.semaphore_wait(barrier, 11)
    halo = pltpu.make_async_remote_copy(
        src_ref=halo_out, dst_ref=halo_in, send_sem=halo_sem.at[0], recv_sem=halo_sem.at[1],
        device_id={"seq": lax.rem(me + 1, 32)}, device_id_type=MESH,
    )
    for i, get in enumerate(chunks):
        for r in (2, 1, 3):
            get.across(r).start()
        if i == 0:
            halo.start()
    for r in (2, 4, 6):
        pl.semaphore_signal(line_sem, inc=1, device_id={"seq": lax.bitwise_xor(me, r)}, device_id_type=MESH)
    pl.semaphore_wait(line_sem, 3)
    pl.semaphore_signal(all_sem, inc=1, device_id={"seq": lax.bitwise_xor(me, 1)}, device_id_type=MESH)

    def picked(raw, pos):
        @pl.loop(0, 8)
        def _(i):
            cols = columns(i, 512)
            pos[:, cols] = jnp.dot(pick_ref[...], raw[:, cols], preferred_element_type=jnp.float32)

    def rimmed(s, pos):
        pos[pl.ds(0, 1), :] = halo32[pl.ds(2 * s, 1), :]
        pos[pl.ds(16, 1), :] = halo32[pl.ds(2 * s + 1, 1), :]

    picked(kv, kp)
    picked(vv, vp)
    halo.wait_recv()
    halo32[...] = jnp.where(me > 0, halo_in[...].astype(jnp.float32), 0.0)
    rimmed(0, kp)
    rimmed(1, vp)
    pl.semaphore_wait(all_sem, 1)
    owners = [lax.div(lang_ref[0, s], 4) for s in range(2)]
    places = [lax.rem(lang_ref[0, s], 4) for s in range(2)]

    def chosen(four, s):
        row = lax.broadcasted_iota(jnp.int32, four.shape, 0)
        return jnp.sum(jnp.where(row == places[s], four.astype(jnp.float32), 0.0), axis=0, keepdims=True)

    def carrier(d, tap_cols, put):
        cols = columns(d)
        taps = [[tap_rows(tsel, (2 * j + n,) * 2, tap_cols) for j in range(3)] for n in range(2)]
        for b in range(8):
            put(b, (short_block(kp, taps[0], b, cols) * short_block(vp, taps[1], b, cols)).astype(jnp.bfloat16))

    def x_copy(r):
        return pltpu.make_async_remote_copy(
            src_ref=send_x.at[r], dst_ref=recv_x.at[pl.ds(pl.multiple_of(me * 16, 16), 16), :],
            send_sem=x_send.at[r], recv_sem=x_recv.at[r],
            device_id={"seq": lax.bitwise_xor(me, r)}, device_id_type=MESH,
        )

    for i in range(4):
        for r in (1, 3, 2):
            chunks[i].across(r).wait_recv()
        for s in range(2):
            for n in range(6):
                tsel[s, pl.ds(n, 1), 1024 * i:1024 * i + 1024] = chosen(tk_all[i][owners[s], n], s)

        @pl.loop(1 if i == 0 else 0, 8)
        def _(k, i=i):
            j, flip = lax.div(k, 2), lax.rem(k, 2)
            r = 8 * j + 2 * lax.bitwise_xor(j, i) + flip

            def put(b, value):
                send_x[r, :, lane(b)] = value

            carrier(lax.bitwise_xor(me, r), columns(8 * i + 2 * j + lax.bitwise_xor(core, flip)), put)
            x_copy(r).start()

        if i == 2:
            loads[4].wait()
            for get in (tq_get, down_get):
                for r in (2, 1, 3) if get is tq_get else (1, 3):
                    get.across(r).start()

    loads[5].wait()
    for r in (3, 1):
        up_get.across(r).start()
    own = pl.ds(pl.multiple_of(me * 16, 16), 16)

    def put_own(b, value):
        recv_x[own, lane(b)] = value

    carrier(me, columns(core), put_own)
    picked(qv, qp)
    rimmed(2, qp)

    for load in loads[6:]:
        load.wait()
    filter_spectrum(filt, table, step, high, low, p, h, tw)
    down_get.across(1).wait_recv()
    down_get.relay(1).start()
    down_get.beside(1).start()

    @pl.loop(1, 32)
    def _(r):
        x_copy(r).wait_recv()

    stage_matmul(p, table, [recv_x])
    spectrum_product(p, h, tw, g)
    skip = skip_ref[pl.ds(me, 1), :]

    def y_copy(r):
        d = lax.bitwise_xor(me, r)
        j = lax.div(r, 8)
        i = lax.bitwise_xor(lax.rem(lax.div(r, 2), 4), j)
        slot = 8 * i + 2 * j + lax.rem(d, 2)
        return pltpu.make_async_remote_copy(
            src_ref=send_y.at[pl.ds(pl.multiple_of(slot * 16, 16), 16), :], dst_ref=recv_y.at[me],
            send_sem=y_send.at[r], recv_sem=y_recv.at[r],
            device_id={"seq": d}, device_id_type=MESH,
        )

    for i in range(0, 4, GROUP):
        blocks = [
            pl.ds(pl.multiple_of(32 * chip_of(i + n, j), 32), 32) for n in range(GROUP) for j in range(4)
        ]

        @pl.loop(0, 4)
        def _(m, i=i, blocks=blocks):
            cols = columns(m, 256)
            left = jnp.concatenate([back[rows, :] for rows in blocks], 0)
            signal = jnp.concatenate([recv_x[rows, cols] for rows in blocks], 0)
            conv = jnp.dot(left, g[:, cols], preferred_element_type=jnp.float32)
            both = jnp.concatenate([skip, skip], 1)
            send_y[128 * i:128 * (i + GROUP), cols] = (conv + both * signal.astype(jnp.float32)).astype(jnp.bfloat16)

        @pl.loop(8 * i + (1 if i == 0 else 0), 8 * (i + GROUP))
        def _(k):
            n, j, flip = lax.div(k, 8), lax.rem(lax.div(k, 2), 4), lax.rem(k, 2)
            y_copy(8 * j + 2 * lax.bitwise_xor(j, n) + flip).start()

    up_get.across(3).wait_recv()
    up_get.relay(3).start()
    up_get.beside(3).start()
    for r in (1, 3, 2):
        tq_get.across(r).wait_recv()
        tq_get.beside(r).start()
    down_get.across(3).wait_recv()
    down_get.beside(3).start()
    up_get.across(1).wait_recv()
    up_get.beside(1).start()
    for r in (1, 3, 2):
        tq_get.beside(r).wait_recv()
    for s in range(2):
        for t in range(3):
            tqsel[s, pl.ds(t, 1), :] = chosen(tq_all[owners[s], t], s)

    @pl.loop(0, 32)
    def _(d):
        cols = columns(d)
        taps = [tap_rows(tqsel, (j, j), cols) for j in range(3)]
        for b in range(8):
            qs[pl.ds(b * 16, 16), cols] = short_block(qp, taps, b, cols).astype(jnp.bfloat16)

    for get in (down_get, up_get):
        get.across(2).wait_recv()
        get.beside(2).start()
    for get in (down_get, up_get):
        for r in (1, 3, 2):
            get.beside(r).wait_recv()
    for s in range(2):
        down2[pl.ds(16 * s, 16), :] = down_all[lang_ref[0, s]]
        up2[pl.ds(16 * s, 16), :] = up_all[lang_ref[0, s]]
    lows = lax.dot_general(
        qs[...], down2[...], (((1,), (1,)), ((), ())), preferred_element_type=jnp.float32
    )
    row_seg = lax.rem(lax.div(lax.broadcasted_iota(jnp.int32, (128, 32), 0), 8), 2)
    col_seg = lax.div(lax.broadcasted_iota(jnp.int32, (128, 32), 1), 16)
    lows = jnp.where(row_seg == col_seg, lows, 0.0).astype(jnp.bfloat16)

    @pl.loop(0, 8)
    def _(i):
        cols = columns(i, 512)
        gate[:, cols] = qs[:, cols].astype(jnp.float32) + jnp.dot(
            lows, up2[:, cols], preferred_element_type=jnp.float32
        )

    recv_y[me] = send_y[pl.ds(pl.multiple_of(core * 16, 16), 16), :]

    def out_copy(i):
        cols = columns(i, 256)
        return pltpu.make_async_copy(out.at[:, cols], out_ref.at[0, :, cols], out_sem.at[i])

    @pl.loop(0, 16)
    def _(k):
        n, j = lax.div(k, 4), lax.rem(k, 4)
        r = 8 * j + 2 * lax.bitwise_xor(j, n)
        chip = lax.bitwise_xor(lax.div(me, 2), lax.div(r, 2))
        cols = columns(chip, 256)

        @pl.when(k > 0)
        def _():
            y_copy(r).wait_recv()

        y_copy(r + 1).wait_recv()
        for one in range(2):
            s = 2 * chip + one
            for b in range(8):
                piece = gate[pl.ds(b * 16, 16), columns(s)] * recv_y[s, :, lane(b)].astype(jnp.float32)
                prod[pl.ds(b * 16, 16), lane(one)] = piece.astype(jnp.bfloat16)
        out[:, cols] = jnp.dot(
            unpick_ref[...], prod[...], preferred_element_type=jnp.float32
        ).astype(jnp.bfloat16)
        out_copy(chip).start()

    halo.wait_send()
    for get in chunks + [tq_get]:
        for r in (1, 2, 3):
            get.across(r).wait_send()
    for r in (1, 2, 3):
        tq_get.beside(r).wait_send()
    for get, way in ((down_get, 1), (up_get, 3)):
        for r in (1, 3):
            get.across(r).wait_send()
        get.relay(way).wait_send()
        for r in (1, 2, 3):
            get.beside(r).wait_send()

    @pl.loop(1, 32)
    def _(r):
        x_copy(r).wait_send()
        y_copy(r).wait_send()

    @pl.loop(0, 16)
    def _(i):
        out_copy(i).wait()


def local(q_stream, k_stream, v_stream, lang_ids, short_taps, adapter_down, adapter_up, long_filter, bypass_coefficient):
    fwd, back, step = dft_tables()
    pick, unpick = pick_tables()
    bf16, f32 = jnp.bfloat16, jnp.float32
    vmem = pl.BlockSpec(memory_space=pltpu.VMEM)
    anywhere = pl.BlockSpec(memory_space=pl.ANY)
    dma = pltpu.SemaphoreType.DMA
    arrays = [
        ((128, 4096), bf16), ((128, 4096), bf16), ((128, 4096), bf16),
        ((160, 4096), f32), ((160, 4096), f32), ((160, 4096), f32),
        ((3, 3, 4, 4096), bf16), ] + [((4, 6, 4, 1024), bf16)] * 4 + [((4, 3, 4, 4096), bf16),
        ((2, 8, 4096), f32), ((2, 8, 4096), f32),
        ((16, 16, 4096), bf16), ((16, 16, 4096), bf16), ((32, 4096), bf16), ((32, 4096), bf16),
        ((8, 4096), f32), ((8, 4096), bf16), ((8, 4096), bf16),
        ((32, 16, 1024), bf16), ((512, 1024), bf16),
        ((4096, 128), f32), ((1024, 512), bf16), ((512, 1024), bf16), ((2, 512, 128), f32),
        ((512, 1024), bf16), ((512, 1024), bf16),
        ((1024, 1024), f32), ((1024, 1024), f32), ((1024, 1024), f32), ((1024, 1024), bf16),
        ((512, 1024), bf16), ((32, 16, 1024), bf16),
        ((128, 4096), bf16), ((128, 4096), f32), ((128, 256), bf16), ((128, 4096), bf16),
    ]
    return pl.pallas_call(
        fused_kernel,
        out_shape=jax.ShapeDtypeStruct(q_stream.shape, bf16),
        in_specs=[pl.BlockSpec(memory_space=pltpu.SMEM)] + [vmem] * 3 + [anywhere] * 10,
        out_specs=anywhere,
        scratch_shapes=[pltpu.VMEM(shape, kind) for shape, kind in arrays]
        + [dma((10,)), dma((2,)), dma((4, 4, 3)), dma((4, 3)), dma((4, 3)), dma((4, 3))]
        + [dma((32,))] * 4
        + [dma((16,)), pltpu.SemaphoreType.REGULAR, pltpu.SemaphoreType.REGULAR],
        compiler_params=pltpu.CompilerParams(
            collective_id=0, has_side_effects=True, vmem_limit_bytes=60 << 20
        ),
    )(
        lang_ids, bypass_coefficient.reshape(32, 128), jnp.asarray(pick), jnp.asarray(unpick),
        q_stream, k_stream, v_stream, short_taps.transpose(1, 2, 0, 3), adapter_down, adapter_up, long_filter,
        jnp.asarray(fwd), jnp.asarray(back), jnp.asarray(step),
    )


def solution(mesh):
    placed = (
        P("lang", "seq", None),
        P("lang", "seq", None),
        P("lang", "seq", None),
        P("lang", "seq"),
        P("lang", None, None, None),
        P("lang", None, None),
        P("lang", None, None),
        P(None, "seq"),
        P(),
    )
    return jax.shard_map(
        local, mesh=mesh, in_specs=placed, out_specs=P("lang", "seq", None), check_vma=False
    )
```

```python
import math

import jax
import jax.numpy as jnp
import ml_dtypes
import numpy as np
from jax import lax
from jax.experimental import pallas as pl
from jax.experimental.pallas import tpu as pltpu
from jax.sharding import PartitionSpec as P

LANES = 128
ROWS = 32


def dft_tables():
    k1 = np.arange(512)[:, None]
    a = np.arange(512)[None, :]
    ang = 2.0 * np.pi * ((2 * k1 + 1) * a % 2048) / 2048.0
    table = np.concatenate([np.cos(ang), -np.sin(ang)], 0).astype(np.float32)
    one = 2.0 * np.pi * (2 * np.arange(512) + 1) / 16384.0
    step = np.stack([np.cos(one), -np.sin(one)]).astype(np.float32)
    step = np.ascontiguousarray(np.broadcast_to(step[:, :, None], (2, 512, LANES)))
    fwd = table.astype(ml_dtypes.bfloat16)
    return fwd, np.ascontiguousarray(fwd.T), step


def cadd(p, q):
    return p[0] + q[0], p[1] + q[1]


def csub(p, q):
    return p[0] - q[0], p[1] - q[1]


def cmul(p, q):
    return p[0] * q[0] - p[1] * q[1], p[0] * q[1] + p[1] * q[0]


def cmul_conj(p, q):
    return p[0] * q[0] + p[1] * q[1], p[1] * q[0] - p[0] * q[1]


def quarter(p, sign):
    return (p[1], -p[0]) if sign > 0 else (-p[1], p[0])


def dft4(z0, z1, z2, z3, sign):
    s0, s1 = cadd(z0, z2), csub(z0, z2)
    s2, s3 = cadd(z1, z3), quarter(csub(z1, z3), sign)
    return cadd(s0, s2), cadd(s1, s3), csub(s0, s2), csub(s1, s3)


def dft8(z, sign):
    half = math.sqrt(0.5)
    even = dft4(z[0], z[2], z[4], z[6], sign)
    odd = dft4(z[1], z[3], z[5], z[7], sign)
    o1, o3 = odd[1], odd[3]
    if sign > 0:
        o1 = ((o1[0] + o1[1]) * half, (o1[1] - o1[0]) * half)
        o3 = ((o3[1] - o3[0]) * half, (o3[0] + o3[1]) * -half)
    else:
        o1 = ((o1[0] - o1[1]) * half, (o1[0] + o1[1]) * half)
        o3 = ((o3[0] + o3[1]) * -half, (o3[0] - o3[1]) * half)
    turned = (odd[0], o1, quarter(odd[2], sign), o3)
    return [cadd(e, o) for e, o in zip(even, turned)] + [csub(e, o) for e, o in zip(even, turned)]


def lane(b):
    return slice(b * LANES, (b + 1) * LANES)


def stage_matmul(out_ref, left_ref, right_refs, width=512):
    columns = out_ref.shape[1]

    @pl.loop(0, columns // width)
    def _(j):
        cols = pl.ds(pl.multiple_of(j * width, width), width)
        total = None
        for right_ref in right_refs:
            term = jnp.dot(left_ref[...], right_ref[:, cols], preferred_element_type=jnp.float32)
            total = term if total is None else total + term
        out_ref[:, cols] = total


def load_points(p_ref, rows_re, rows_im):
    return [(p_ref[rows_re, lane(b)], p_ref[rows_im, lane(b)]) for b in range(8)]


def filter_spectrum(filt_ref, table_ref, step_ref, high_ref, low_ref, p_ref, h_ref, tw_ref):
    for b in range(8):
        @pl.loop(0, 4)
        def _(i):
            rows = filt_ref[pl.ds(i * 1024 + b, 128, stride=8), :]
            high = rows.astype(jnp.bfloat16)
            at = pl.ds(pl.multiple_of(i * 128, 128), 128)
            high_ref[at, lane(b)] = high
            low_ref[at, lane(b)] = (rows - high.astype(jnp.float32)).astype(jnp.bfloat16)
    stage_matmul(p_ref, table_ref, [high_ref, low_ref])

    @pl.loop(0, 512 // ROWS)
    def _(i):
        re = pl.ds(pl.multiple_of(i * ROWS, ROWS), ROWS)
        im = pl.ds(pl.multiple_of(512 + i * ROWS, ROWS), ROWS)
        points = load_points(p_ref, re, im)
        step = (step_ref[0, re, :], step_ref[1, re, :])
        turn = step
        for b in range(1, 8):
            tw_ref[re, lane(b)] = turn[0]
            tw_ref[im, lane(b)] = turn[1]
            points[b] = cmul(points[b], turn)
            if b < 7:
                turn = cmul(turn, step)
        for k2, value in enumerate(dft8(points, 1)):
            h_ref[re, lane(k2)] = value[0] * (2.0 / 8192.0)
            h_ref[im, lane(k2)] = value[1] * (2.0 / 8192.0)


def spectrum_product(p_ref, h_ref, tw_ref, g_ref):
    @pl.loop(0, 512 // ROWS)
    def _(i):
        re = pl.ds(pl.multiple_of(i * ROWS, ROWS), ROWS)
        im = pl.ds(pl.multiple_of(512 + i * ROWS, ROWS), ROWS)
        points = load_points(p_ref, re, im)
        for b in range(1, 8):
            points[b] = cmul(points[b], (tw_ref[re, lane(b)], tw_ref[im, lane(b)]))
        spec = dft8(points, 1)
        spec = [cmul(v, (h_ref[re, lane(k)], h_ref[im, lane(k)])) for k, v in enumerate(spec)]
        back = dft8(spec, -1)
        for b in range(8):
            value = back[b]
            if b > 0:
                value = cmul_conj(value, (tw_ref[re, lane(b)], tw_ref[im, lane(b)]))
            g_ref[re, lane(b)] = value[0].astype(jnp.bfloat16)
            g_ref[im, lane(b)] = value[1].astype(jnp.bfloat16)


MESH = pl.DeviceIdType.MESH
GROUP = 2


def pick_tables():
    pick = np.zeros((160, 128), np.float32)
    back = np.zeros((128, 128), np.float32)
    for b in range(-2, 8):
        for a in range(16):
            t = 8 * a + b
            if t >= 0:
                pick[(b + 2) * 16 + a, t] = 1.0
                if b >= 0:
                    back[t, b * 16 + a] = 1.0
    return pick.astype(ml_dtypes.bfloat16), back.astype(ml_dtypes.bfloat16)


class Panels:
    def __init__(self, part, sems, y, me):
        self.part, self.sems, self.y, self.me = part, sems, y, me

    def move(self, owner, kind, r, device):
        ref = self.part(owner)
        return pltpu.make_async_remote_copy(
            src_ref=ref, dst_ref=ref, send_sem=self.sems.at[kind, r - 1], recv_sem=self.sems.at[kind + 1, r - 1],
            device_id=device, device_id_type=MESH,
        )

    def across(self, r):
        return self.move(self.y, 0, r, {"lang": lax.rem(self.y + r, 4)})

    def relay(self, r):
        return self.move(lax.rem(self.y + 4 - r, 4), 0, 2, {"lang": lax.rem(self.y + r, 4)})

    def beside(self, r):
        return self.move(lax.rem(self.y + 4 - r, 4), 2, r, {"seq": lax.bitwise_xor(self.me, 1)})


def columns(d, width=LANES):
    return pl.ds(pl.multiple_of(d * width, width), width)


def tap_rows(sel_ref, rows, cols):
    return jnp.concatenate(
        [jnp.broadcast_to(sel_ref[s, pl.ds(rows[s], 1), cols], (8, LANES)) for s in range(2)], 0
    )


def short_block(pos_ref, taps, b, cols):
    total = None
    for j in range(3):
        term = pos_ref[pl.ds((b + 2 - j) * 16, 16), cols] * taps[j]
        total = term if total is None else total + term
    return total


def fused_kernel(
    lang_ref, skip_ref, pick_ref, unpick_ref, q_in, k_in, v_in, taps_in, down_in, up_in, filt_in, table_in,
    back_in, step_in, out_ref,
    qv, kv, vv, qp, kp, vp, traw, tk_0, tk_1, tk_2, tk_3, tq_all, tsel, tqsel, down_all, up_all, down2, up2,
    halo32, halo_out, halo_in, send_x, recv_x, filt, table, back, step, high, low, p, h, tw, g, send_y, recv_y,
    qs, gate, prod, out, back_sent, local_sem, halo_sem, tk_sem, tq_sem, down_sem, up_sem, x_send, x_recv, y_send, y_recv,
    out_sem, line_sem, all_sem,
):
    y = lax.axis_index("lang")
    me = lax.axis_index("seq")
    core = lax.rem(me, 2)
    tk_all = [tk_0, tk_1, tk_2, tk_3]
    loads = [
        pltpu.make_async_copy(src, dst, local_sem.at[i])
        for i, (src, dst) in enumerate([
            (taps_in, traw), (k_in.at[0], kv), (v_in.at[0], vv), (q_in.at[0], qv),
            (down_in, down_all.at[pl.ds(4 * y, 4)]), (up_in, up_all.at[pl.ds(4 * y, 4)]),
            (filt_in, filt), (table_in, table), (back_in, back), (step_in, step),
        ])
    ]
    for load in loads:
        load.start()

    barrier = pltpu.get_barrier_semaphore()
    for r in range(1, 4):
        pl.semaphore_signal(barrier, inc=1, device_id={"lang": lax.rem(y + r, 4)}, device_id_type=MESH)
    for r in (1, 2, 4, 6, 8, 16, 24):
        pl.semaphore_signal(barrier, inc=1, device_id={"seq": lax.bitwise_xor(me, r)}, device_id_type=MESH)
    pl.semaphore_signal(barrier, inc=1, device_id={"seq": lax.rem(me + 31, 32)}, device_id_type=MESH)

    def chip_of(i, j):
        return lax.bitwise_xor(lax.div(me, 2), 4 * j + lax.bitwise_xor(j, i))

    halves = pl.ds(pl.multiple_of(core * 2048, 2048), 2048)
    chunks = [
        Panels(lambda owner, i=i: tk_all[i].at[owner], tk_sem.at[i], y, me) for i in range(4)
    ]
    tq_get = Panels(lambda owner: tq_all.at[owner, :, :, halves], tq_sem, y, me)
    down_get = Panels(lambda owner: down_all.at[pl.ds(4 * owner + 2 * core, 2)], down_sem, y, me)
    up_get = Panels(lambda owner: up_all.at[pl.ds(4 * owner + 2 * core, 2)], up_sem, y, me)

    loads[0].wait()
    for i in range(4):
        for j in range(4):
            cols = columns(chip_of(i, j), 256)
            for t in range(3):
                for n in range(2):
                    tk_all[i][y, 2 * t + n, :, 256 * j:256 * j + 256] = traw[t, n + 1, :, cols]
    for t in range(3):
        tq_all[y, t] = traw[t, 0]

    halo32[...] = jnp.zeros_like(halo32)
    for s, (load, raw) in enumerate([(loads[1], kv), (loads[2], vv), (loads[3], qv)]):
        load.wait()
        halo32[pl.ds(2 * s, 2), :] = raw[112:128, :].astype(jnp.float32)[14:16]
    halo_out[...] = halo32[...].astype(jnp.bfloat16)

    pl.semaphore_wait(barrier, 11)
    halo = pltpu.make_async_remote_copy(
        src_ref=halo_out, dst_ref=halo_in, send_sem=halo_sem.at[0], recv_sem=halo_sem.at[1],
        device_id={"seq": lax.rem(me + 1, 32)}, device_id_type=MESH,
    )
    for i, get in enumerate(chunks):
        for r in (2, 1, 3):
            get.across(r).start()
        if i == 0:
            halo.start()
    for r in (2, 4, 6):
        pl.semaphore_signal(line_sem, inc=1, device_id={"seq": lax.bitwise_xor(me, r)}, device_id_type=MESH)
    pl.semaphore_wait(line_sem, 3)
    pl.semaphore_signal(all_sem, inc=1, device_id={"seq": lax.bitwise_xor(me, 1)}, device_id_type=MESH)

    def picked(raw, pos):
        @pl.loop(0, 8)
        def _(i):
            cols = columns(i, 512)
            pos[:, cols] = jnp.dot(pick_ref[...], raw[:, cols], preferred_element_type=jnp.float32)

    def rimmed(s, pos):
        pos[pl.ds(0, 1), :] = halo32[pl.ds(2 * s, 1), :]
        pos[pl.ds(16, 1), :] = halo32[pl.ds(2 * s + 1, 1), :]

    picked(kv, kp)
    picked(vv, vp)
    halo.wait_recv()
    halo32[...] = jnp.where(me > 0, halo_in[...].astype(jnp.float32), 0.0)
    rimmed(0, kp)
    rimmed(1, vp)
    pl.semaphore_wait(all_sem, 1)
    owners = [lax.div(lang_ref[0, s], 4) for s in range(2)]
    places = [lax.rem(lang_ref[0, s], 4) for s in range(2)]

    def chosen(four, s):
        row = lax.broadcasted_iota(jnp.int32, four.shape, 0)
        return jnp.sum(jnp.where(row == places[s], four.astype(jnp.float32), 0.0), axis=0, keepdims=True)

    def carrier(d, tap_cols, put):
        cols = columns(d)
        taps = [[tap_rows(tsel, (2 * j + n,) * 2, tap_cols) for j in range(3)] for n in range(2)]
        for b in range(8):
            put(b, (short_block(kp, taps[0], b, cols) * short_block(vp, taps[1], b, cols)).astype(jnp.bfloat16))

    def x_copy(r):
        return pltpu.make_async_remote_copy(
            src_ref=send_x.at[r], dst_ref=recv_x.at[pl.ds(pl.multiple_of(me * 16, 16), 16), :],
            send_sem=x_send.at[r], recv_sem=x_recv.at[r],
            device_id={"seq": lax.bitwise_xor(me, r)}, device_id_type=MESH,
        )

    for i in range(4):
        for r in (1, 3, 2):
            chunks[i].across(r).wait_recv()
        for s in range(2):
            for n in range(6):
                tsel[s, pl.ds(n, 1), 1024 * i:1024 * i + 1024] = chosen(tk_all[i][owners[s], n], s)

        @pl.loop(1 if i == 0 else 0, 8)
        def _(k, i=i):
            j, flip = lax.div(k, 2), lax.rem(k, 2)
            r = 8 * j + 2 * lax.bitwise_xor(j, i) + flip

            def put(b, value):
                send_x[r, :, lane(b)] = value

            carrier(lax.bitwise_xor(me, r), columns(8 * i + 2 * j + lax.bitwise_xor(core, flip)), put)
            x_copy(r).start()

        if i == 2:
            loads[4].wait()
            for get in (tq_get, down_get):
                for r in (2, 1, 3) if get is tq_get else (1, 3):
                    get.across(r).start()

    loads[5].wait()
    for r in (3, 1):
        up_get.across(r).start()
    own = pl.ds(pl.multiple_of(me * 16, 16), 16)

    def put_own(b, value):
        recv_x[own, lane(b)] = value

    carrier(me, columns(core), put_own)
    picked(qv, qp)
    rimmed(2, qp)

    for load in loads[6:]:
        load.wait()
    filter_spectrum(filt, table, step, high, low, p, h, tw)
    for n in range(16):
        rows = pl.ds(pl.multiple_of(32 * chip_of(n // 4, n % 4), 32), 32)
        back_sent[32 * n:32 * n + 32, :] = back[rows, :]

    down_get.across(1).wait_recv()
    down_get.relay(1).start()
    down_get.beside(1).start()

    @pl.loop(1, 32)
    def _(r):
        x_copy(r).wait_recv()

    stage_matmul(p, table, [recv_x])
    spectrum_product(p, h, tw, g)
    skip = skip_ref[pl.ds(me, 1), :]

    def y_copy(r):
        d = lax.bitwise_xor(me, r)
        j = lax.div(r, 8)
        i = lax.bitwise_xor(lax.rem(lax.div(r, 2), 4), j)
        slot = 8 * i + 2 * j + lax.rem(d, 2)
        return pltpu.make_async_remote_copy(
            src_ref=send_y.at[pl.ds(pl.multiple_of(slot * 16, 16), 16), :], dst_ref=recv_y.at[me],
            send_sem=y_send.at[r], recv_sem=y_recv.at[r],
            device_id={"seq": d}, device_id_type=MESH,
        )

    for i in range(0, 4, GROUP):
        @pl.loop(0, 2)
        def _(m, i=i):
            cols = columns(m, 512)
            both = jnp.concatenate([skip] * 4, 1)
            conv = jnp.dot(
                back_sent[128 * i:128 * (i + GROUP), :], g[:, cols], preferred_element_type=jnp.float32
            )
            for n in range(4 * GROUP):
                rows = pl.ds(pl.multiple_of(32 * chip_of(i + n // 4, n % 4), 32), 32)
                send_y[128 * i + 32 * n:128 * i + 32 * n + 32, cols] = (
                    conv[32 * n:32 * n + 32] + both * recv_x[rows, cols].astype(jnp.float32)
                ).astype(jnp.bfloat16)

        @pl.loop(8 * i + (1 if i == 0 else 0), 8 * (i + GROUP))
        def _(k):
            n, j, flip = lax.div(k, 8), lax.rem(lax.div(k, 2), 4), lax.rem(k, 2)
            y_copy(8 * j + 2 * lax.bitwise_xor(j, n) + flip).start()

    up_get.across(3).wait_recv()
    up_get.relay(3).start()
    up_get.beside(3).start()
    for r in (1, 3, 2):
        tq_get.across(r).wait_recv()
        tq_get.beside(r).start()
    down_get.across(3).wait_recv()
    down_get.beside(3).start()
    up_get.across(1).wait_recv()
    up_get.beside(1).start()
    for r in (1, 3, 2):
        tq_get.beside(r).wait_recv()
    for s in range(2):
        for t in range(3):
            tqsel[s, pl.ds(t, 1), :] = chosen(tq_all[owners[s], t], s)

    @pl.loop(0, 32)
    def _(d):
        cols = columns(d)
        taps = [tap_rows(tqsel, (j, j), cols) for j in range(3)]
        for b in range(8):
            qs[pl.ds(b * 16, 16), cols] = short_block(qp, taps, b, cols).astype(jnp.bfloat16)

    for get in (down_get, up_get):
        get.across(2).wait_recv()
        get.beside(2).start()
    for get in (down_get, up_get):
        for r in (1, 3, 2):
            get.beside(r).wait_recv()
    for s in range(2):
        down2[pl.ds(16 * s, 16), :] = down_all[lang_ref[0, s]]
        up2[pl.ds(16 * s, 16), :] = up_all[lang_ref[0, s]]
    lows = lax.dot_general(
        qs[...], down2[...], (((1,), (1,)), ((), ())), preferred_element_type=jnp.float32
    )
    row_seg = lax.rem(lax.div(lax.broadcasted_iota(jnp.int32, (128, 32), 0), 8), 2)
    col_seg = lax.div(lax.broadcasted_iota(jnp.int32, (128, 32), 1), 16)
    lows = jnp.where(row_seg == col_seg, lows, 0.0).astype(jnp.bfloat16)

    @pl.loop(0, 8)
    def _(i):
        cols = columns(i, 512)
        gate[:, cols] = qs[:, cols].astype(jnp.float32) + jnp.dot(
            lows, up2[:, cols], preferred_element_type=jnp.float32
        )

    recv_y[me] = send_y[pl.ds(pl.multiple_of(core * 16, 16), 16), :]

    def out_copy(i):
        cols = columns(i, 256)
        return pltpu.make_async_copy(out.at[:, cols], out_ref.at[0, :, cols], out_sem.at[i])

    @pl.loop(0, 16)
    def _(k):
        n, j = lax.div(k, 4), lax.rem(k, 4)
        r = 8 * j + 2 * lax.bitwise_xor(j, n)
        chip = lax.bitwise_xor(lax.div(me, 2), lax.div(r, 2))
        cols = columns(chip, 256)

        @pl.when(k > 0)
        def _():
            y_copy(r).wait_recv()

        y_copy(r + 1).wait_recv()
        for one in range(2):
            s = 2 * chip + one
            for b in range(8):
                piece = gate[pl.ds(b * 16, 16), columns(s)] * recv_y[s, :, lane(b)].astype(jnp.float32)
                prod[pl.ds(b * 16, 16), lane(one)] = piece.astype(jnp.bfloat16)
        out[:, cols] = jnp.dot(
            unpick_ref[...], prod[...], preferred_element_type=jnp.float32
        ).astype(jnp.bfloat16)
        out_copy(chip).start()

    halo.wait_send()
    for get in chunks + [tq_get]:
        for r in (1, 2, 3):
            get.across(r).wait_send()
    for r in (1, 2, 3):
        tq_get.beside(r).wait_send()
    for get, way in ((down_get, 1), (up_get, 3)):
        for r in (1, 3):
            get.across(r).wait_send()
        get.relay(way).wait_send()
        for r in (1, 2, 3):
            get.beside(r).wait_send()

    @pl.loop(1, 32)
    def _(r):
        x_copy(r).wait_send()
        y_copy(r).wait_send()

    @pl.loop(0, 16)
    def _(i):
        out_copy(i).wait()


def local(q_stream, k_stream, v_stream, lang_ids, short_taps, adapter_down, adapter_up, long_filter, bypass_coefficient):
    fwd, back, step = dft_tables()
    pick, unpick = pick_tables()
    bf16, f32 = jnp.bfloat16, jnp.float32
    vmem = pl.BlockSpec(memory_space=pltpu.VMEM)
    anywhere = pl.BlockSpec(memory_space=pl.ANY)
    dma = pltpu.SemaphoreType.DMA
    arrays = [
        ((128, 4096), bf16), ((128, 4096), bf16), ((128, 4096), bf16),
        ((160, 4096), f32), ((160, 4096), f32), ((160, 4096), f32),
        ((3, 3, 4, 4096), bf16), ] + [((4, 6, 4, 1024), bf16)] * 4 + [((4, 3, 4, 4096), bf16),
        ((2, 8, 4096), f32), ((2, 8, 4096), f32),
        ((16, 16, 4096), bf16), ((16, 16, 4096), bf16), ((32, 4096), bf16), ((32, 4096), bf16),
        ((8, 4096), f32), ((8, 4096), bf16), ((8, 4096), bf16),
        ((32, 16, 1024), bf16), ((512, 1024), bf16),
        ((4096, 128), f32), ((1024, 512), bf16), ((512, 1024), bf16), ((2, 512, 128), f32),
        ((512, 1024), bf16), ((512, 1024), bf16),
        ((1024, 1024), f32), ((1024, 1024), f32), ((1024, 1024), f32), ((1024, 1024), bf16),
        ((512, 1024), bf16), ((32, 16, 1024), bf16),
        ((128, 4096), bf16), ((128, 4096), f32), ((128, 256), bf16), ((128, 4096), bf16), ((512, 1024), bf16),
    ]
    return pl.pallas_call(
        fused_kernel,
        out_shape=jax.ShapeDtypeStruct(q_stream.shape, bf16),
        in_specs=[pl.BlockSpec(memory_space=pltpu.SMEM)] + [vmem] * 3 + [anywhere] * 10,
        out_specs=anywhere,
        scratch_shapes=[pltpu.VMEM(shape, kind) for shape, kind in arrays]
        + [dma((10,)), dma((2,)), dma((4, 4, 3)), dma((4, 3)), dma((4, 3)), dma((4, 3))]
        + [dma((32,))] * 4
        + [dma((16,)), pltpu.SemaphoreType.REGULAR, pltpu.SemaphoreType.REGULAR],
        compiler_params=pltpu.CompilerParams(
            collective_id=0, has_side_effects=True, vmem_limit_bytes=60 << 20
        ),
    )(
        lang_ids, bypass_coefficient.reshape(32, 128), jnp.asarray(pick), jnp.asarray(unpick),
        q_stream, k_stream, v_stream, short_taps.transpose(1, 2, 0, 3), adapter_down, adapter_up, long_filter,
        jnp.asarray(fwd), jnp.asarray(back), jnp.asarray(step),
    )


def solution(mesh):
    placed = (
        P("lang", "seq", None),
        P("lang", "seq", None),
        P("lang", "seq", None),
        P("lang", "seq"),
        P("lang", None, None, None),
        P("lang", None, None),
        P("lang", None, None),
        P(None, "seq"),
        P(),
    )
    return jax.shard_map(
        local, mesh=mesh, in_specs=placed, out_specs=P("lang", "seq", None), check_vma=False
    )
```

```python
import math

import jax
import jax.numpy as jnp
import ml_dtypes
import numpy as np
from jax import lax
from jax.experimental import pallas as pl
from jax.experimental.pallas import tpu as pltpu
from jax.sharding import PartitionSpec as P

LANES = 128
ROWS = 32


def dft_tables():
    k1 = np.arange(512)[:, None]
    a = np.arange(512)[None, :]
    ang = 2.0 * np.pi * ((2 * k1 + 1) * a % 2048) / 2048.0
    table = np.concatenate([np.cos(ang), -np.sin(ang)], 0).astype(np.float32)
    one = 2.0 * np.pi * (2 * np.arange(512) + 1) / 16384.0
    step = np.stack([np.cos(one), -np.sin(one)]).astype(np.float32)
    step = np.ascontiguousarray(np.broadcast_to(step[:, :, None], (2, 512, LANES)))
    fwd = table.astype(ml_dtypes.bfloat16)
    return fwd, np.ascontiguousarray(fwd.T), step


def cadd(p, q):
    return p[0] + q[0], p[1] + q[1]


def csub(p, q):
    return p[0] - q[0], p[1] - q[1]


def cmul(p, q):
    return p[0] * q[0] - p[1] * q[1], p[0] * q[1] + p[1] * q[0]


def cmul_conj(p, q):
    return p[0] * q[0] + p[1] * q[1], p[1] * q[0] - p[0] * q[1]


def quarter(p, sign):
    return (p[1], -p[0]) if sign > 0 else (-p[1], p[0])


def dft4(z0, z1, z2, z3, sign):
    s0, s1 = cadd(z0, z2), csub(z0, z2)
    s2, s3 = cadd(z1, z3), quarter(csub(z1, z3), sign)
    return cadd(s0, s2), cadd(s1, s3), csub(s0, s2), csub(s1, s3)


def dft8(z, sign):
    half = math.sqrt(0.5)
    even = dft4(z[0], z[2], z[4], z[6], sign)
    odd = dft4(z[1], z[3], z[5], z[7], sign)
    o1, o3 = odd[1], odd[3]
    if sign > 0:
        o1 = ((o1[0] + o1[1]) * half, (o1[1] - o1[0]) * half)
        o3 = ((o3[1] - o3[0]) * half, (o3[0] + o3[1]) * -half)
    else:
        o1 = ((o1[0] - o1[1]) * half, (o1[0] + o1[1]) * half)
        o3 = ((o3[0] + o3[1]) * -half, (o3[0] - o3[1]) * half)
    turned = (odd[0], o1, quarter(odd[2], sign), o3)
    return [cadd(e, o) for e, o in zip(even, turned)] + [csub(e, o) for e, o in zip(even, turned)]


def lane(b):
    return slice(b * LANES, (b + 1) * LANES)


def stage_matmul(out_ref, left_ref, right_refs, width=1024):
    columns = out_ref.shape[1]

    @pl.loop(0, columns // width)
    def _(j):
        cols = pl.ds(pl.multiple_of(j * width, width), width)
        total = None
        for right_ref in right_refs:
            term = jnp.dot(left_ref[...], right_ref[:, cols], preferred_element_type=jnp.float32)
            total = term if total is None else total + term
        out_ref[:, cols] = total


def load_points(p_ref, rows_re, rows_im):
    return [(p_ref[rows_re, lane(b)], p_ref[rows_im, lane(b)]) for b in range(8)]


def filter_spectrum(filt_ref, table_ref, step_ref, high_ref, low_ref, p_ref, h_ref, tw_ref):
    for b in range(8):
        @pl.loop(0, 4)
        def _(i):
            rows = filt_ref[pl.ds(i * 1024 + b, 128, stride=8), :]
            high = rows.astype(jnp.bfloat16)
            at = pl.ds(pl.multiple_of(i * 128, 128), 128)
            high_ref[at, lane(b)] = high
            low_ref[at, lane(b)] = (rows - high.astype(jnp.float32)).astype(jnp.bfloat16)
    stage_matmul(p_ref, table_ref, [high_ref, low_ref])

    @pl.loop(0, 512 // ROWS)
    def _(i):
        re = pl.ds(pl.multiple_of(i * ROWS, ROWS), ROWS)
        im = pl.ds(pl.multiple_of(512 + i * ROWS, ROWS), ROWS)
        points = load_points(p_ref, re, im)
        step = (step_ref[0, re, :], step_ref[1, re, :])
        turn = step
        for b in range(1, 8):
            tw_ref[re, lane(b)] = turn[0]
            tw_ref[im, lane(b)] = turn[1]
            points[b] = cmul(points[b], turn)
            if b < 7:
                turn = cmul(turn, step)
        for k2, value in enumerate(dft8(points, 1)):
            h_ref[re, lane(k2)] = value[0] * (2.0 / 8192.0)
            h_ref[im, lane(k2)] = value[1] * (2.0 / 8192.0)


def spectrum_product(p_ref, h_ref, tw_ref, g_ref):
    @pl.loop(0, 512 // ROWS)
    def _(i):
        re = pl.ds(pl.multiple_of(i * ROWS, ROWS), ROWS)
        im = pl.ds(pl.multiple_of(512 + i * ROWS, ROWS), ROWS)
        points = load_points(p_ref, re, im)
        for b in range(1, 8):
            points[b] = cmul(points[b], (tw_ref[re, lane(b)], tw_ref[im, lane(b)]))
        spec = dft8(points, 1)
        spec = [cmul(v, (h_ref[re, lane(k)], h_ref[im, lane(k)])) for k, v in enumerate(spec)]
        back = dft8(spec, -1)
        for b in range(8):
            value = back[b]
            if b > 0:
                value = cmul_conj(value, (tw_ref[re, lane(b)], tw_ref[im, lane(b)]))
            g_ref[re, lane(b)] = value[0].astype(jnp.bfloat16)
            g_ref[im, lane(b)] = value[1].astype(jnp.bfloat16)


MESH = pl.DeviceIdType.MESH


def pick_tables():
    pick = np.zeros((160, 128), np.float32)
    back = np.zeros((128, 128), np.float32)
    for b in range(-2, 8):
        for a in range(16):
            t = 8 * a + b
            if t >= 0:
                pick[(b + 2) * 16 + a, t] = 1.0
                if b >= 0:
                    back[t, b * 16 + a] = 1.0
    return pick.astype(ml_dtypes.bfloat16), back.astype(ml_dtypes.bfloat16)


class Panels:
    def __init__(self, part, sems, y, me):
        self.part, self.sems, self.y, self.me = part, sems, y, me

    def move(self, owner, kind, r, device):
        ref = self.part(owner)
        return pltpu.make_async_remote_copy(
            src_ref=ref, dst_ref=ref, send_sem=self.sems.at[kind, r - 1], recv_sem=self.sems.at[kind + 1, r - 1],
            device_id=device, device_id_type=MESH,
        )

    def across(self, r):
        return self.move(self.y, 0, r, {"lang": lax.rem(self.y + r, 4)})

    def relay(self, r):
        return self.move(lax.rem(self.y + 4 - r, 4), 0, 2, {"lang": lax.rem(self.y + r, 4)})

    def beside(self, r):
        return self.move(lax.rem(self.y + 4 - r, 4), 2, r, {"seq": lax.bitwise_xor(self.me, 1)})


def columns(d, width=LANES):
    return pl.ds(pl.multiple_of(d * width, width), width)


def tap_rows(sel_ref, rows, cols):
    return jnp.concatenate(
        [jnp.broadcast_to(sel_ref[s, pl.ds(rows[s], 1), cols], (8, LANES)) for s in range(2)], 0
    )


def short_block(pos_ref, taps, b, cols):
    total = None
    for j in range(3):
        term = pos_ref[pl.ds((b + 2 - j) * 16, 16), cols] * taps[j]
        total = term if total is None else total + term
    return total


def fused_kernel(
    lang_ref, skip_in, pick_in, unpick_in, q_in, k_in, v_in, taps_in, down_in, up_in, filt_in, table_in,
    back_in, step_in, out_ref,
    qv, kv, vv, qp, kp, vp, traw, tk_0, tk_1, tk_2, tk_3, tq_all, tsel, tqsel, down_all, up_all, down2, up2,
    halo32, halo_out, halo_in, send_x, recv_x, filt, table, back, step, high, low, p, h, tw, g, send_y, recv_y,
    qs, gate, prod, out, back_sent, skip_ref, pick_ref, unpick_ref, local_sem, halo_sem, tk_sem, tq_sem, down_sem, up_sem, x_send, x_recv, y_send, y_recv,
    out_sem, line_sem, all_sem,
):
    y = lax.axis_index("lang")
    me = lax.axis_index("seq")
    core = lax.rem(me, 2)
    tk_all = [tk_0, tk_1, tk_2, tk_3]
    loads = [
        pltpu.make_async_copy(src, dst, local_sem.at[i])
        for i, (src, dst) in enumerate([
            (taps_in, traw), (k_in.at[0], kv), (v_in.at[0], vv), (q_in.at[0], qv),
            (down_in, down_all.at[pl.ds(4 * y, 4)]), (up_in, up_all.at[pl.ds(4 * y, 4)]),
            (filt_in, filt), (table_in, table), (back_in, back), (step_in, step),
            (skip_in, skip_ref), (unpick_in, unpick_ref), (pick_in, pick_ref),
        ])
    ]
    loads[0].start()

    barrier = pltpu.get_barrier_semaphore()
    for r in range(1, 4):
        pl.semaphore_signal(barrier, inc=1, device_id={"lang": lax.rem(y + r, 4)}, device_id_type=MESH)
    for r in (1, 2, 4, 6, 8, 16, 24):
        pl.semaphore_signal(barrier, inc=1, device_id={"seq": lax.bitwise_xor(me, r)}, device_id_type=MESH)
    pl.semaphore_signal(barrier, inc=1, device_id={"seq": lax.rem(me + 31, 32)}, device_id_type=MESH)
    for load in loads[1:4] + loads[12:] + loads[4:12]:
        load.start()

    def chip_of(i, j):
        return lax.bitwise_xor(lax.div(me, 2), 4 * j + lax.bitwise_xor(j, i))

    halves = pl.ds(pl.multiple_of(core * 2048, 2048), 2048)
    chunks = [
        Panels(lambda owner, i=i: tk_all[i].at[owner], tk_sem.at[i], y, me) for i in range(4)
    ]
    tq_get = Panels(lambda owner: tq_all.at[owner, :, :, halves], tq_sem, y, me)
    down_get = Panels(lambda owner: down_all.at[pl.ds(4 * owner + 2 * core, 2)], down_sem, y, me)
    up_get = Panels(lambda owner: up_all.at[pl.ds(4 * owner + 2 * core, 2)], up_sem, y, me)

    loads[0].wait()
    for i in range(4):
        for j in range(4):
            cols = columns(chip_of(i, j), 256)
            for t in range(3):
                for n in range(2):
                    tk_all[i][y, 2 * t + n, :, 256 * j:256 * j + 256] = traw[t, n + 1, :, cols]
    for t in range(3):
        tq_all[y, t] = traw[t, 0]

    halo32[...] = jnp.zeros_like(halo32)
    for s, (load, raw) in enumerate([(loads[1], kv), (loads[2], vv), (loads[3], qv)]):
        load.wait()
        halo32[pl.ds(2 * s, 2), :] = raw[112:128, :].astype(jnp.float32)[14:16]
    halo_out[...] = halo32[...].astype(jnp.bfloat16)

    pl.semaphore_wait(barrier, 11)
    halo = pltpu.make_async_remote_copy(
        src_ref=halo_out, dst_ref=halo_in, send_sem=halo_sem.at[0], recv_sem=halo_sem.at[1],
        device_id={"seq": lax.rem(me + 1, 32)}, device_id_type=MESH,
    )
    for i, get in enumerate(chunks):
        for r in (2, 1, 3):
            get.across(r).start()
        if i == 0:
            halo.start()
    for r in (2, 4, 6):
        pl.semaphore_signal(line_sem, inc=1, device_id={"seq": lax.bitwise_xor(me, r)}, device_id_type=MESH)
    pl.semaphore_wait(line_sem, 3)
    pl.semaphore_signal(all_sem, inc=1, device_id={"seq": lax.bitwise_xor(me, 1)}, device_id_type=MESH)

    def picked(raw, pos):
        @pl.loop(0, 8)
        def _(i):
            cols = columns(i, 512)
            pos[:, cols] = jnp.dot(pick_ref[...], raw[:, cols], preferred_element_type=jnp.float32)

    def rimmed(s, pos):
        pos[pl.ds(0, 1), :] = halo32[pl.ds(2 * s, 1), :]
        pos[pl.ds(16, 1), :] = halo32[pl.ds(2 * s + 1, 1), :]

    loads[12].wait()
    picked(kv, kp)
    picked(vv, vp)
    halo.wait_recv()
    halo32[...] = jnp.where(me > 0, halo_in[...].astype(jnp.float32), 0.0)
    rimmed(0, kp)
    rimmed(1, vp)
    pl.semaphore_wait(all_sem, 1)
    owners = [lax.div(lang_ref[0, s], 4) for s in range(2)]
    places = [lax.rem(lang_ref[0, s], 4) for s in range(2)]

    def chosen(four, s):
        row = lax.broadcasted_iota(jnp.int32, four.shape, 0)
        return jnp.sum(jnp.where(row == places[s], four.astype(jnp.float32), 0.0), axis=0, keepdims=True)

    def carrier(d, tap_cols, put):
        cols = columns(d)
        taps = [[tap_rows(tsel, (2 * j + n,) * 2, tap_cols) for j in range(3)] for n in range(2)]
        for b in range(8):
            put(b, (short_block(kp, taps[0], b, cols) * short_block(vp, taps[1], b, cols)).astype(jnp.bfloat16))

    def x_copy(r):
        return pltpu.make_async_remote_copy(
            src_ref=send_x.at[r], dst_ref=recv_x.at[pl.ds(pl.multiple_of(me * 16, 16), 16), :],
            send_sem=x_send.at[r], recv_sem=x_recv.at[r],
            device_id={"seq": lax.bitwise_xor(me, r)}, device_id_type=MESH,
        )

    for i in range(4):
        for r in (1, 3, 2):
            chunks[i].across(r).wait_recv()
        for s in range(2):
            for n in range(6):
                tsel[s, pl.ds(n, 1), 1024 * i:1024 * i + 1024] = chosen(tk_all[i][owners[s], n], s)

        @pl.loop(1 if i == 0 else 0, 8)
        def _(k, i=i):
            j, flip = lax.div(k, 2), lax.rem(k, 2)
            r = 8 * j + 2 * lax.bitwise_xor(j, i) + flip

            def put(b, value):
                send_x[r, :, lane(b)] = value

            carrier(lax.bitwise_xor(me, r), columns(8 * i + 2 * j + lax.bitwise_xor(core, flip)), put)
            x_copy(r).start()

        if i == 2:
            loads[4].wait()
            for get in (tq_get, down_get):
                for r in (2, 1, 3) if get is tq_get else (1, 3):
                    get.across(r).start()

    loads[5].wait()
    for r in (3, 1):
        up_get.across(r).start()
    own = pl.ds(pl.multiple_of(me * 16, 16), 16)

    def put_own(b, value):
        recv_x[own, lane(b)] = value

    carrier(me, columns(core), put_own)
    picked(qv, qp)
    rimmed(2, qp)

    for load in loads[6:12]:
        load.wait()
    filter_spectrum(filt, table, step, high, low, p, h, tw)
    for n in range(16):
        rows = pl.ds(pl.multiple_of(32 * chip_of(n // 4, n % 4), 32), 32)
        back_sent[32 * n:32 * n + 32, :] = back[rows, :]

    down_get.across(1).wait_recv()
    down_get.relay(1).start()
    down_get.beside(1).start()

    @pl.loop(1, 32)
    def _(r):
        x_copy(r).wait_recv()

    stage_matmul(p, table, [recv_x])
    spectrum_product(p, h, tw, g)
    skip = skip_ref[pl.ds(me, 1), :]

    def y_copy(r):
        d = lax.bitwise_xor(me, r)
        j = lax.div(r, 8)
        i = lax.bitwise_xor(lax.rem(lax.div(r, 2), 4), j)
        slot = 8 * i + 2 * j + lax.rem(d, 2)
        return pltpu.make_async_remote_copy(
            src_ref=send_y.at[pl.ds(pl.multiple_of(slot * 16, 16), 16), :], dst_ref=recv_y.at[me],
            send_sem=y_send.at[r], recv_sem=y_recv.at[r],
            device_id={"seq": d}, device_id_type=MESH,
        )

    for i, group in ((0, 1), (1, 3)):
        @pl.loop(0, 2)
        def _(m, i=i):
            cols = columns(m, 512)
            both = jnp.concatenate([skip] * 4, 1)
            conv = jnp.dot(
                back_sent[128 * i:128 * (i + group), :], g[:, cols], preferred_element_type=jnp.float32
            )
            for n in range(4 * group):
                rows = pl.ds(pl.multiple_of(32 * chip_of(i + n // 4, n % 4), 32), 32)
                send_y[128 * i + 32 * n:128 * i + 32 * n + 32, cols] = (
                    conv[32 * n:32 * n + 32] + both * recv_x[rows, cols].astype(jnp.float32)
                ).astype(jnp.bfloat16)

        @pl.loop(8 * i + (1 if i == 0 else 0), 8 * (i + group))
        def _(k):
            n, j, flip = lax.div(k, 8), lax.rem(lax.div(k, 2), 4), lax.rem(k, 2)
            y_copy(8 * j + 2 * lax.bitwise_xor(j, n) + flip).start()

    up_get.across(3).wait_recv()
    up_get.relay(3).start()
    up_get.beside(3).start()
    for r in (1, 3, 2):
        tq_get.across(r).wait_recv()
        tq_get.beside(r).start()
    down_get.across(3).wait_recv()
    down_get.beside(3).start()
    up_get.across(1).wait_recv()
    up_get.beside(1).start()
    for r in (1, 3, 2):
        tq_get.beside(r).wait_recv()
    for s in range(2):
        for t in range(3):
            tqsel[s, pl.ds(t, 1), :] = chosen(tq_all[owners[s], t], s)

    @pl.loop(0, 32)
    def _(d):
        cols = columns(d)
        taps = [tap_rows(tqsel, (j, j), cols) for j in range(3)]
        for b in range(8):
            qs[pl.ds(b * 16, 16), cols] = short_block(qp, taps, b, cols).astype(jnp.bfloat16)

    for get in (down_get, up_get):
        get.across(2).wait_recv()
        get.beside(2).start()
    for get in (down_get, up_get):
        for r in (1, 3, 2):
            get.beside(r).wait_recv()
    for s in range(2):
        down2[pl.ds(16 * s, 16), :] = down_all[lang_ref[0, s]]
        up2[pl.ds(16 * s, 16), :] = up_all[lang_ref[0, s]]
    lows = lax.dot_general(
        qs[...], down2[...], (((1,), (1,)), ((), ())), preferred_element_type=jnp.float32
    )
    row_seg = lax.rem(lax.div(lax.broadcasted_iota(jnp.int32, (128, 32), 0), 8), 2)
    col_seg = lax.div(lax.broadcasted_iota(jnp.int32, (128, 32), 1), 16)
    lows = jnp.where(row_seg == col_seg, lows, 0.0).astype(jnp.bfloat16)

    @pl.loop(0, 8)
    def _(i):
        cols = columns(i, 512)
        gate[:, cols] = qs[:, cols].astype(jnp.float32) + jnp.dot(
            lows, up2[:, cols], preferred_element_type=jnp.float32
        )

    recv_y[me] = send_y[pl.ds(pl.multiple_of(core * 16, 16), 16), :]

    halo.wait_send()
    for get in chunks + [tq_get]:
        for r in (1, 2, 3):
            get.across(r).wait_send()
    for r in (1, 2, 3):
        tq_get.beside(r).wait_send()
    for get, way in ((down_get, 1), (up_get, 3)):
        for r in (1, 3):
            get.across(r).wait_send()
        get.relay(way).wait_send()
        for r in (1, 2, 3):
            get.beside(r).wait_send()

    @pl.loop(1, 32)
    def _(r):
        x_copy(r).wait_send()

    def out_copy(i):
        cols = columns(i, 256)
        return pltpu.make_async_copy(out.at[:, cols], out_ref.at[0, :, cols], out_sem.at[i])

    @pl.loop(0, 16)
    def _(k):
        n, j = lax.div(k, 4), lax.rem(k, 4)
        r = 8 * j + 2 * lax.bitwise_xor(j, n)
        chip = lax.bitwise_xor(lax.div(me, 2), lax.div(r, 2))
        cols = columns(chip, 256)

        @pl.when(k > 0)
        def _():
            y_copy(r).wait_recv()

        y_copy(r + 1).wait_recv()
        for one in range(2):
            s = 2 * chip + one
            for b in range(8):
                piece = gate[pl.ds(b * 16, 16), columns(s)] * recv_y[s, :, lane(b)].astype(jnp.float32)
                prod[pl.ds(b * 16, 16), lane(one)] = piece.astype(jnp.bfloat16)
        out[:, cols] = jnp.dot(
            unpick_ref[...], prod[...], preferred_element_type=jnp.float32
        ).astype(jnp.bfloat16)
        out_copy(chip).start()

        @pl.when(k > 0)
        def _():
            y_copy(r).wait_send()

        y_copy(r + 1).wait_send()

    @pl.loop(0, 16)
    def _(i):
        out_copy(i).wait()


def local(q_stream, k_stream, v_stream, lang_ids, short_taps, adapter_down, adapter_up, long_filter, bypass_coefficient):
    fwd, back, step = dft_tables()
    pick, unpick = pick_tables()
    bf16, f32 = jnp.bfloat16, jnp.float32
    anywhere = pl.BlockSpec(memory_space=pl.ANY)
    dma = pltpu.SemaphoreType.DMA
    arrays = [
        ((128, 4096), bf16), ((128, 4096), bf16), ((128, 4096), bf16),
        ((160, 4096), f32), ((160, 4096), f32), ((160, 4096), f32),
        ((3, 3, 4, 4096), bf16), ] + [((4, 6, 4, 1024), bf16)] * 4 + [((4, 3, 4, 4096), bf16),
        ((2, 8, 4096), f32), ((2, 8, 4096), f32),
        ((16, 16, 4096), bf16), ((16, 16, 4096), bf16), ((32, 4096), bf16), ((32, 4096), bf16),
        ((8, 4096), f32), ((8, 4096), bf16), ((8, 4096), bf16),
        ((32, 16, 1024), bf16), ((512, 1024), bf16),
        ((4096, 128), f32), ((1024, 512), bf16), ((512, 1024), bf16), ((2, 512, 128), f32),
        ((512, 1024), bf16), ((512, 1024), bf16),
        ((1024, 1024), f32), ((1024, 1024), f32), ((1024, 1024), f32), ((1024, 1024), bf16),
        ((512, 1024), bf16), ((32, 16, 1024), bf16),
        ((128, 4096), bf16), ((128, 4096), f32), ((128, 256), bf16), ((128, 4096), bf16), ((512, 1024), bf16),
        ((32, 128), f32), ((160, 128), bf16), ((128, 128), bf16),
    ]
    return pl.pallas_call(
        fused_kernel,
        out_shape=jax.ShapeDtypeStruct(q_stream.shape, bf16),
        in_specs=[pl.BlockSpec(memory_space=pltpu.SMEM)] + [anywhere] * 13,
        out_specs=anywhere,
        scratch_shapes=[pltpu.VMEM(shape, kind) for shape, kind in arrays]
        + [dma((13,)), dma((2,)), dma((4, 4, 3)), dma((4, 3)), dma((4, 3)), dma((4, 3))]
        + [dma((32,))] * 4
        + [dma((16,)), pltpu.SemaphoreType.REGULAR, pltpu.SemaphoreType.REGULAR],
        compiler_params=pltpu.CompilerParams(
            collective_id=0, has_side_effects=True, vmem_limit_bytes=60 << 20
        ),
    )(
        lang_ids, bypass_coefficient.reshape(32, 128), jnp.asarray(pick), jnp.asarray(unpick),
        q_stream, k_stream, v_stream, short_taps.transpose(1, 2, 0, 3), adapter_down, adapter_up, long_filter,
        jnp.asarray(fwd), jnp.asarray(back), jnp.asarray(step),
    )


def solution(mesh):
    placed = (
        P("lang", "seq", None),
        P("lang", "seq", None),
        P("lang", "seq", None),
        P("lang", "seq"),
        P("lang", None, None, None),
        P("lang", None, None),
        P("lang", None, None),
        P(None, "seq"),
        P(),
    )
    return jax.shard_map(
        local, mesh=mesh, in_specs=placed, out_specs=P("lang", "seq", None), check_vma=False
    )
```

```python
import math

import jax
import jax.numpy as jnp
import ml_dtypes
import numpy as np
from jax import lax
from jax.experimental import pallas as pl
from jax.experimental.pallas import tpu as pltpu
from jax.sharding import PartitionSpec as P

LANES = 128
ROWS = 32


def dft_tables():
    k1 = np.arange(512)[:, None]
    a = np.arange(512)[None, :]
    ang = 2.0 * np.pi * ((2 * k1 + 1) * a % 2048) / 2048.0
    table = np.concatenate([np.cos(ang), -np.sin(ang)], 0).astype(np.float32)
    one = 2.0 * np.pi * (2 * np.arange(512) + 1) / 16384.0
    step = np.stack([np.cos(one), -np.sin(one)]).astype(np.float32)
    step = np.ascontiguousarray(np.broadcast_to(step[:, :, None], (2, 512, LANES)))
    fwd = table.astype(ml_dtypes.bfloat16)
    return fwd, np.ascontiguousarray(fwd.T), step


def cadd(p, q):
    return p[0] + q[0], p[1] + q[1]


def csub(p, q):
    return p[0] - q[0], p[1] - q[1]


def cmul(p, q):
    return p[0] * q[0] - p[1] * q[1], p[0] * q[1] + p[1] * q[0]


def cmul_conj(p, q):
    return p[0] * q[0] + p[1] * q[1], p[1] * q[0] - p[0] * q[1]


def quarter(p, sign):
    return (p[1], -p[0]) if sign > 0 else (-p[1], p[0])


def dft4(z0, z1, z2, z3, sign):
    s0, s1 = cadd(z0, z2), csub(z0, z2)
    s2, s3 = cadd(z1, z3), quarter(csub(z1, z3), sign)
    return cadd(s0, s2), cadd(s1, s3), csub(s0, s2), csub(s1, s3)


def dft8(z, sign):
    half = math.sqrt(0.5)
    even = dft4(z[0], z[2], z[4], z[6], sign)
    odd = dft4(z[1], z[3], z[5], z[7], sign)
    o1, o3 = odd[1], odd[3]
    if sign > 0:
        o1 = ((o1[0] + o1[1]) * half, (o1[1] - o1[0]) * half)
        o3 = ((o3[1] - o3[0]) * half, (o3[0] + o3[1]) * -half)
    else:
        o1 = ((o1[0] - o1[1]) * half, (o1[0] + o1[1]) * half)
        o3 = ((o3[0] + o3[1]) * -half, (o3[0] - o3[1]) * half)
    turned = (odd[0], o1, quarter(odd[2], sign), o3)
    return [cadd(e, o) for e, o in zip(even, turned)] + [csub(e, o) for e, o in zip(even, turned)]


def lane(b):
    return slice(b * LANES, (b + 1) * LANES)


def stage_matmul(out_ref, left_ref, right_refs, width=1024):
    columns = out_ref.shape[1]

    @pl.loop(0, columns // width)
    def _(j):
        cols = pl.ds(pl.multiple_of(j * width, width), width)
        total = None
        for right_ref in right_refs:
            term = jnp.dot(left_ref[...], right_ref[:, cols], preferred_element_type=jnp.float32)
            total = term if total is None else total + term
        out_ref[:, cols] = total


def load_points(p_ref, rows_re, rows_im):
    return [(p_ref[rows_re, lane(b)], p_ref[rows_im, lane(b)]) for b in range(8)]


def filter_spectrum(filt_ref, table_ref, step_ref, high_ref, low_ref, p_ref, h_ref, tw_ref):
    for b in range(8):
        @pl.loop(0, 4)
        def _(i):
            rows = filt_ref[pl.ds(i * 1024 + b, 128, stride=8), :]
            high = rows.astype(jnp.bfloat16)
            at = pl.ds(pl.multiple_of(i * 128, 128), 128)
            high_ref[at, lane(b)] = high
            low_ref[at, lane(b)] = (rows - high.astype(jnp.float32)).astype(jnp.bfloat16)
    stage_matmul(p_ref, table_ref, [high_ref, low_ref])

    @pl.loop(0, 512 // ROWS)
    def _(i):
        re = pl.ds(pl.multiple_of(i * ROWS, ROWS), ROWS)
        im = pl.ds(pl.multiple_of(512 + i * ROWS, ROWS), ROWS)
        points = load_points(p_ref, re, im)
        step = (step_ref[0, re, :], step_ref[1, re, :])
        turn = step
        for b in range(1, 8):
            tw_ref[re, lane(b)] = turn[0]
            tw_ref[im, lane(b)] = turn[1]
            points[b] = cmul(points[b], turn)
            if b < 7:
                turn = cmul(turn, step)
        for k2, value in enumerate(dft8(points, 1)):
            h_ref[re, lane(k2)] = value[0] * (2.0 / 8192.0)
            h_ref[im, lane(k2)] = value[1] * (2.0 / 8192.0)


def spectrum_product(p_ref, h_ref, tw_ref, g_ref):
    @pl.loop(0, 512 // ROWS)
    def _(i):
        re = pl.ds(pl.multiple_of(i * ROWS, ROWS), ROWS)
        im = pl.ds(pl.multiple_of(512 + i * ROWS, ROWS), ROWS)
        points = load_points(p_ref, re, im)
        for b in range(1, 8):
            points[b] = cmul(points[b], (tw_ref[re, lane(b)], tw_ref[im, lane(b)]))
        spec = dft8(points, 1)
        spec = [cmul(v, (h_ref[re, lane(k)], h_ref[im, lane(k)])) for k, v in enumerate(spec)]
        back = dft8(spec, -1)
        for b in range(8):
            value = back[b]
            if b > 0:
                value = cmul_conj(value, (tw_ref[re, lane(b)], tw_ref[im, lane(b)]))
            g_ref[re, lane(b)] = value[0].astype(jnp.bfloat16)
            g_ref[im, lane(b)] = value[1].astype(jnp.bfloat16)


MESH = pl.DeviceIdType.MESH


def pick_tables():
    pick = np.zeros((160, 128), np.float32)
    back = np.zeros((128, 128), np.float32)
    for b in range(-2, 8):
        for a in range(16):
            t = 8 * a + b
            if t >= 0:
                pick[(b + 2) * 16 + a, t] = 1.0
                if b >= 0:
                    back[t, b * 16 + a] = 1.0
    return pick.astype(ml_dtypes.bfloat16), back.astype(ml_dtypes.bfloat16)


class Panels:
    def __init__(self, part, sems, y, me):
        self.part, self.sems, self.y, self.me = part, sems, y, me

    def move(self, owner, kind, r, device):
        ref = self.part(owner)
        return pltpu.make_async_remote_copy(
            src_ref=ref, dst_ref=ref, send_sem=self.sems.at[kind, r - 1], recv_sem=self.sems.at[kind + 1, r - 1],
            device_id=device, device_id_type=MESH,
        )

    def across(self, r):
        return self.move(self.y, 0, r, {"lang": lax.rem(self.y + r, 4)})

    def relay(self, r):
        return self.move(lax.rem(self.y + 4 - r, 4), 0, 2, {"lang": lax.rem(self.y + r, 4)})

    def beside(self, r):
        return self.move(lax.rem(self.y + 4 - r, 4), 2, r, {"seq": lax.bitwise_xor(self.me, 1)})


def columns(d, width=LANES):
    return pl.ds(pl.multiple_of(d * width, width), width)


def tap_rows(sel_ref, rows, cols):
    return jnp.concatenate(
        [jnp.broadcast_to(sel_ref[s, pl.ds(rows[s], 1), cols], (8, LANES)) for s in range(2)], 0
    )


def short_block(pos_ref, taps, b, cols):
    total = None
    for j in range(3):
        term = pos_ref[pl.ds((b + 2 - j) * 16, 16), cols] * taps[j]
        total = term if total is None else total + term
    return total


def fused_kernel(
    lang_ref, skip_in, pick_in, unpick_in, q_in, k_in, v_in, taps_in, down_in, up_in, filt_in, table_in,
    back_in, step_in, out_ref,
    qv, kv, vv, qp, kp, vp, traw, tk_0, tk_1, tk_2, tk_3, tq_all, tsel, tqsel, down_all, up_all, down2, up2,
    halo32, halo_out, halo_in, send_x, recv_x, filt, table, back, step, high, low, p, h, tw, g, send_y, recv_y,
    qs, gate, prod, out, back_sent, skip_ref, pick_ref, unpick_ref, local_sem, halo_sem, tk_sem, tq_sem, down_sem, up_sem, x_send, x_recv, y_send, y_recv,
    out_sem, line_sem, all_sem,
):
    y = lax.axis_index("lang")
    me = lax.axis_index("seq")
    core = lax.rem(me, 2)
    tk_all = [tk_0, tk_1, tk_2, tk_3]
    loads = [
        pltpu.make_async_copy(src, dst, local_sem.at[i])
        for i, (src, dst) in enumerate([
            (taps_in, traw), (k_in.at[0], kv), (v_in.at[0], vv), (q_in.at[0], qv),
            (down_in, down_all.at[pl.ds(4 * y, 4)]), (up_in, up_all.at[pl.ds(4 * y, 4)]),
            (filt_in, filt), (table_in, table), (back_in, back), (step_in, step),
            (skip_in, skip_ref), (unpick_in, unpick_ref), (pick_in, pick_ref),
        ])
    ]
    loads[0].start()

    barrier = pltpu.get_barrier_semaphore()
    for r in range(1, 4):
        pl.semaphore_signal(barrier, inc=1, device_id={"lang": lax.rem(y + r, 4)}, device_id_type=MESH)
    for r in (1, 2, 4, 6, 8, 16, 24):
        pl.semaphore_signal(barrier, inc=1, device_id={"seq": lax.bitwise_xor(me, r)}, device_id_type=MESH)
    pl.semaphore_signal(barrier, inc=1, device_id={"seq": lax.rem(me + 31, 32)}, device_id_type=MESH)
    for load in loads[1:4] + loads[12:] + loads[4:12]:
        load.start()

    def chip_of(i, j):
        return lax.bitwise_xor(lax.div(me, 2), 4 * j + lax.bitwise_xor(j, i))

    halves = pl.ds(pl.multiple_of(core * 2048, 2048), 2048)
    chunks = [
        Panels(lambda owner, i=i: tk_all[i].at[owner], tk_sem.at[i], y, me) for i in range(4)
    ]
    tq_get = Panels(lambda owner: tq_all.at[owner, :, :, halves], tq_sem, y, me)
    down_get = Panels(lambda owner: down_all.at[pl.ds(4 * owner + 2 * core, 2)], down_sem, y, me)
    up_get = Panels(lambda owner: up_all.at[pl.ds(4 * owner + 2 * core, 2)], up_sem, y, me)

    loads[0].wait()
    for i in range(4):
        for j in range(4):
            cols = columns(chip_of(i, j), 256)
            for t in range(3):
                for n in range(2):
                    tk_all[i][y, 2 * t + n, :, 256 * j:256 * j + 256] = traw[t, n + 1, :, cols]
    for t in range(3):
        tq_all[y, t] = traw[t, 0]

    halo32[...] = jnp.zeros_like(halo32)
    for s, (load, raw) in enumerate([(loads[1], kv), (loads[2], vv), (loads[3], qv)]):
        load.wait()
        halo32[pl.ds(2 * s, 2), :] = raw[112:128, :].astype(jnp.float32)[14:16]
    halo_out[...] = halo32[...].astype(jnp.bfloat16)

    pl.semaphore_wait(barrier, 11)
    halo = pltpu.make_async_remote_copy(
        src_ref=halo_out, dst_ref=halo_in, send_sem=halo_sem.at[0], recv_sem=halo_sem.at[1],
        device_id={"seq": lax.rem(me + 1, 32)}, device_id_type=MESH,
    )
    for i, get in enumerate(chunks):
        for r in (2, 1, 3):
            get.across(r).start()
        if i == 0:
            halo.start()
    for r in (2, 4, 6):
        pl.semaphore_signal(line_sem, inc=1, device_id={"seq": lax.bitwise_xor(me, r)}, device_id_type=MESH)
    pl.semaphore_wait(line_sem, 3)
    pl.semaphore_signal(all_sem, inc=1, device_id={"seq": lax.bitwise_xor(me, 1)}, device_id_type=MESH)

    def picked(raw, pos):
        @pl.loop(0, 8)
        def _(i):
            cols = columns(i, 512)
            pos[:, cols] = jnp.dot(pick_ref[...], raw[:, cols], preferred_element_type=jnp.float32)

    def rimmed(s, pos):
        pos[pl.ds(0, 1), :] = halo32[pl.ds(2 * s, 1), :]
        pos[pl.ds(16, 1), :] = halo32[pl.ds(2 * s + 1, 1), :]

    loads[12].wait()
    picked(kv, kp)
    picked(vv, vp)
    halo.wait_recv()
    halo32[...] = jnp.where(me > 0, halo_in[...].astype(jnp.float32), 0.0)
    rimmed(0, kp)
    rimmed(1, vp)
    pl.semaphore_wait(all_sem, 1)
    owners = [lax.div(lang_ref[0, s], 4) for s in range(2)]
    places = [lax.rem(lang_ref[0, s], 4) for s in range(2)]

    def chosen(four, s):
        row = lax.broadcasted_iota(jnp.int32, four.shape, 0)
        return jnp.sum(jnp.where(row == places[s], four.astype(jnp.float32), 0.0), axis=0, keepdims=True)

    def carrier(d, tap_cols, put):
        cols = columns(d)
        taps = [[tap_rows(tsel, (2 * j + n,) * 2, tap_cols) for j in range(3)] for n in range(2)]
        for b in range(8):
            put(b, (short_block(kp, taps[0], b, cols) * short_block(vp, taps[1], b, cols)).astype(jnp.bfloat16))

    def x_copy(r):
        return pltpu.make_async_remote_copy(
            src_ref=send_x.at[r], dst_ref=recv_x.at[pl.ds(pl.multiple_of(me * 16, 16), 16), :],
            send_sem=x_send.at[r], recv_sem=x_recv.at[r],
            device_id={"seq": lax.bitwise_xor(me, r)}, device_id_type=MESH,
        )

    for i in range(4):
        for r in (1, 3, 2):
            chunks[i].across(r).wait_recv()
        for s in range(2):
            for n in range(6):
                tsel[s, pl.ds(n, 1), 1024 * i:1024 * i + 1024] = chosen(tk_all[i][owners[s], n], s)

        @pl.loop(1 if i == 0 else 0, 8)
        def _(k, i=i):
            j, flip = lax.div(k, 2), lax.rem(k, 2)
            r = 8 * j + 2 * lax.bitwise_xor(j, i) + flip

            def put(b, value):
                send_x[r, :, lane(b)] = value

            carrier(lax.bitwise_xor(me, r), columns(8 * i + 2 * j + lax.bitwise_xor(core, flip)), put)
            x_copy(r).start()

        if i == 2:
            loads[4].wait()
            for get in (tq_get, down_get):
                for r in (2, 1, 3) if get is tq_get else (1, 3):
                    get.across(r).start()

    loads[5].wait()
    for r in (3, 1):
        up_get.across(r).start()
    own = pl.ds(pl.multiple_of(me * 16, 16), 16)

    def put_own(b, value):
        recv_x[own, lane(b)] = value

    carrier(me, columns(core), put_own)
    picked(qv, qp)
    rimmed(2, qp)

    for load in loads[6:12]:
        load.wait()
    filter_spectrum(filt, table, step, high, low, p, h, tw)
    for n in range(16):
        rows = pl.ds(pl.multiple_of(32 * chip_of(n // 4, n % 4), 32), 32)
        back_sent[32 * n:32 * n + 32, :] = back[rows, :]

    down_get.across(1).wait_recv()
    down_get.relay(1).start()
    down_get.beside(1).start()

    @pl.loop(1, 32)
    def _(r):
        x_copy(r).wait_recv()

    stage_matmul(p, table, [recv_x])
    spectrum_product(p, h, tw, g)
    skip = skip_ref[pl.ds(me, 1), :]

    def y_copy(r):
        d = lax.bitwise_xor(me, r)
        j = lax.div(r, 8)
        i = lax.bitwise_xor(lax.rem(lax.div(r, 2), 4), j)
        slot = 8 * i + 2 * j + lax.rem(d, 2)
        return pltpu.make_async_remote_copy(
            src_ref=send_y.at[pl.ds(pl.multiple_of(slot * 16, 16), 16), :], dst_ref=recv_y.at[me],
            send_sem=y_send.at[r], recv_sem=y_recv.at[r],
            device_id={"seq": d}, device_id_type=MESH,
        )

    for i, group in ((0, 1), (1, 3)):
        @pl.loop(0, 1)
        def _(m, i=i):
            cols = columns(m, 1024)
            both = jnp.concatenate([skip] * 8, 1)
            conv = jnp.dot(
                back_sent[128 * i:128 * (i + group), :], g[:, cols], preferred_element_type=jnp.float32
            )
            for n in range(4 * group):
                rows = pl.ds(pl.multiple_of(32 * chip_of(i + n // 4, n % 4), 32), 32)
                send_y[128 * i + 32 * n:128 * i + 32 * n + 32, cols] = (
                    conv[32 * n:32 * n + 32] + both * recv_x[rows, cols].astype(jnp.float32)
                ).astype(jnp.bfloat16)

        @pl.loop(8 * i + (1 if i == 0 else 0), 8 * (i + group))
        def _(k):
            n, j, flip = lax.div(k, 8), lax.rem(lax.div(k, 2), 4), lax.rem(k, 2)
            y_copy(8 * j + 2 * lax.bitwise_xor(j, n) + flip).start()

    up_get.across(3).wait_recv()
    up_get.relay(3).start()
    up_get.beside(3).start()
    for r in (1, 3, 2):
        tq_get.across(r).wait_recv()
        tq_get.beside(r).start()
    down_get.across(3).wait_recv()
    down_get.beside(3).start()
    up_get.across(1).wait_recv()
    up_get.beside(1).start()
    for r in (1, 3, 2):
        tq_get.beside(r).wait_recv()
    for s in range(2):
        for t in range(3):
            tqsel[s, pl.ds(t, 1), :] = chosen(tq_all[owners[s], t], s)

    @pl.loop(0, 32)
    def _(d):
        cols = columns(d)
        taps = [tap_rows(tqsel, (j, j), cols) for j in range(3)]
        for b in range(8):
            qs[pl.ds(b * 16, 16), cols] = short_block(qp, taps, b, cols).astype(jnp.bfloat16)

    for get in (down_get, up_get):
        get.across(2).wait_recv()
        get.beside(2).start()
    for get in (down_get, up_get):
        for r in (1, 3, 2):
            get.beside(r).wait_recv()
    for s in range(2):
        down2[pl.ds(16 * s, 16), :] = down_all[lang_ref[0, s]]
        up2[pl.ds(16 * s, 16), :] = up_all[lang_ref[0, s]]
    lows = lax.dot_general(
        qs[...], down2[...], (((1,), (1,)), ((), ())), preferred_element_type=jnp.float32
    )
    row_seg = lax.rem(lax.div(lax.broadcasted_iota(jnp.int32, (128, 32), 0), 8), 2)
    col_seg = lax.div(lax.broadcasted_iota(jnp.int32, (128, 32), 1), 16)
    lows = jnp.where(row_seg == col_seg, lows, 0.0).astype(jnp.bfloat16)

    @pl.loop(0, 8)
    def _(i):
        cols = columns(i, 512)
        gate[:, cols] = qs[:, cols].astype(jnp.float32) + jnp.dot(
            lows, up2[:, cols], preferred_element_type=jnp.float32
        )

    recv_y[me] = send_y[pl.ds(pl.multiple_of(core * 16, 16), 16), :]

    halo.wait_send()
    for get in chunks + [tq_get]:
        for r in (1, 2, 3):
            get.across(r).wait_send()
    for r in (1, 2, 3):
        tq_get.beside(r).wait_send()
    for get, way in ((down_get, 1), (up_get, 3)):
        for r in (1, 3):
            get.across(r).wait_send()
        get.relay(way).wait_send()
        for r in (1, 2, 3):
            get.beside(r).wait_send()

    @pl.loop(1, 32)
    def _(r):
        x_copy(r).wait_send()

    def out_copy(i):
        cols = columns(i, 256)
        return pltpu.make_async_copy(out.at[:, cols], out_ref.at[0, :, cols], out_sem.at[i])

    @pl.loop(0, 16)
    def _(k):
        n, j = lax.div(k, 4), lax.rem(k, 4)
        r = 8 * j + 2 * lax.bitwise_xor(j, n)
        chip = lax.bitwise_xor(lax.div(me, 2), lax.div(r, 2))
        cols = columns(chip, 256)

        @pl.when(k > 0)
        def _():
            y_copy(r).wait_recv()

        y_copy(r + 1).wait_recv()
        for one in range(2):
            s = 2 * chip + one
            for b in range(8):
                piece = gate[pl.ds(b * 16, 16), columns(s)] * recv_y[s, :, lane(b)].astype(jnp.float32)
                prod[pl.ds(b * 16, 16), lane(one)] = piece.astype(jnp.bfloat16)
        out[:, cols] = jnp.dot(
            unpick_ref[...], prod[...], preferred_element_type=jnp.float32
        ).astype(jnp.bfloat16)
        out_copy(chip).start()

        @pl.when(k > 0)
        def _():
            y_copy(r).wait_send()

        y_copy(r + 1).wait_send()

    @pl.loop(0, 16)
    def _(i):
        out_copy(i).wait()


def local(q_stream, k_stream, v_stream, lang_ids, short_taps, adapter_down, adapter_up, long_filter, bypass_coefficient):
    fwd, back, step = dft_tables()
    pick, unpick = pick_tables()
    bf16, f32 = jnp.bfloat16, jnp.float32
    anywhere = pl.BlockSpec(memory_space=pl.ANY)
    dma = pltpu.SemaphoreType.DMA
    arrays = [
        ((128, 4096), bf16), ((128, 4096), bf16), ((128, 4096), bf16),
        ((160, 4096), f32), ((160, 4096), f32), ((160, 4096), f32),
        ((3, 3, 4, 4096), bf16), ] + [((4, 6, 4, 1024), bf16)] * 4 + [((4, 3, 4, 4096), bf16),
        ((2, 8, 4096), f32), ((2, 8, 4096), f32),
        ((16, 16, 4096), bf16), ((16, 16, 4096), bf16), ((32, 4096), bf16), ((32, 4096), bf16),
        ((8, 4096), f32), ((8, 4096), bf16), ((8, 4096), bf16),
        ((32, 16, 1024), bf16), ((512, 1024), bf16),
        ((4096, 128), f32), ((1024, 512), bf16), ((512, 1024), bf16), ((2, 512, 128), f32),
        ((512, 1024), bf16), ((512, 1024), bf16),
        ((1024, 1024), f32), ((1024, 1024), f32), ((1024, 1024), f32), ((1024, 1024), bf16),
        ((512, 1024), bf16), ((32, 16, 1024), bf16),
        ((128, 4096), bf16), ((128, 4096), f32), ((128, 256), bf16), ((128, 4096), bf16), ((512, 1024), bf16),
        ((32, 128), f32), ((160, 128), bf16), ((128, 128), bf16),
    ]
    return pl.pallas_call(
        fused_kernel,
        out_shape=jax.ShapeDtypeStruct(q_stream.shape, bf16),
        in_specs=[pl.BlockSpec(memory_space=pltpu.SMEM)] + [anywhere] * 13,
        out_specs=anywhere,
        scratch_shapes=[pltpu.VMEM(shape, kind) for shape, kind in arrays]
        + [dma((13,)), dma((2,)), dma((4, 4, 3)), dma((4, 3)), dma((4, 3)), dma((4, 3))]
        + [dma((32,))] * 4
        + [dma((16,)), pltpu.SemaphoreType.REGULAR, pltpu.SemaphoreType.REGULAR],
        compiler_params=pltpu.CompilerParams(
            collective_id=0, has_side_effects=True, vmem_limit_bytes=60 << 20
        ),
    )(
        lang_ids, bypass_coefficient.reshape(32, 128), jnp.asarray(pick), jnp.asarray(unpick),
        q_stream, k_stream, v_stream, short_taps.transpose(1, 2, 0, 3), adapter_down, adapter_up, long_filter,
        jnp.asarray(fwd), jnp.asarray(back), jnp.asarray(step),
    )


def solution(mesh):
    placed = (
        P("lang", "seq", None),
        P("lang", "seq", None),
        P("lang", "seq", None),
        P("lang", "seq"),
        P("lang", None, None, None),
        P("lang", None, None),
        P("lang", None, None),
        P(None, "seq"),
        P(),
    )
    return jax.shard_map(
        local, mesh=mesh, in_specs=placed, out_specs=P("lang", "seq", None), check_vma=False
    )
```

```python
import math

import jax
import jax.numpy as jnp
import ml_dtypes
import numpy as np
from jax import lax
from jax.experimental import pallas as pl
from jax.experimental.pallas import tpu as pltpu
from jax.sharding import PartitionSpec as P

LANES = 128
ROWS = 32


def dft_tables():
    k1 = np.arange(512)[:, None]
    a = np.arange(512)[None, :]
    ang = 2.0 * np.pi * ((2 * k1 + 1) * a % 2048) / 2048.0
    table = np.concatenate([np.cos(ang), -np.sin(ang)], 0).astype(np.float32)
    one = 2.0 * np.pi * (2 * np.arange(512) + 1) / 16384.0
    step = np.stack([np.cos(one), -np.sin(one)]).astype(np.float32)
    step = np.ascontiguousarray(np.broadcast_to(step[:, :, None], (2, 512, LANES)))
    fwd = table.astype(ml_dtypes.bfloat16)
    return fwd, np.ascontiguousarray(fwd.T), step


def cadd(p, q):
    return p[0] + q[0], p[1] + q[1]


def csub(p, q):
    return p[0] - q[0], p[1] - q[1]


def cmul(p, q):
    return p[0] * q[0] - p[1] * q[1], p[0] * q[1] + p[1] * q[0]


def cmul_conj(p, q):
    return p[0] * q[0] + p[1] * q[1], p[1] * q[0] - p[0] * q[1]


def quarter(p, sign):
    return (p[1], -p[0]) if sign > 0 else (-p[1], p[0])


def dft4(z0, z1, z2, z3, sign):
    s0, s1 = cadd(z0, z2), csub(z0, z2)
    s2, s3 = cadd(z1, z3), quarter(csub(z1, z3), sign)
    return cadd(s0, s2), cadd(s1, s3), csub(s0, s2), csub(s1, s3)


def dft8(z, sign):
    half = math.sqrt(0.5)
    even = dft4(z[0], z[2], z[4], z[6], sign)
    odd = dft4(z[1], z[3], z[5], z[7], sign)
    o1, o3 = odd[1], odd[3]
    if sign > 0:
        o1 = ((o1[0] + o1[1]) * half, (o1[1] - o1[0]) * half)
        o3 = ((o3[1] - o3[0]) * half, (o3[0] + o3[1]) * -half)
    else:
        o1 = ((o1[0] - o1[1]) * half, (o1[0] + o1[1]) * half)
        o3 = ((o3[0] + o3[1]) * -half, (o3[0] - o3[1]) * half)
    turned = (odd[0], o1, quarter(odd[2], sign), o3)
    return [cadd(e, o) for e, o in zip(even, turned)] + [csub(e, o) for e, o in zip(even, turned)]


def lane(b):
    return slice(b * LANES, (b + 1) * LANES)


def stage_matmul(out_ref, left_ref, right_refs, width=1024):
    columns = out_ref.shape[1]

    @pl.loop(0, columns // width)
    def _(j):
        cols = pl.ds(pl.multiple_of(j * width, width), width)
        total = None
        for right_ref in right_refs:
            term = jnp.dot(left_ref[...], right_ref[:, cols], preferred_element_type=jnp.float32)
            total = term if total is None else total + term
        out_ref[:, cols] = total


def load_points(p_ref, rows_re, rows_im):
    return [(p_ref[rows_re, lane(b)], p_ref[rows_im, lane(b)]) for b in range(8)]


def filter_spectrum(filt_ref, table_ref, step_ref, high_ref, low_ref, p_ref, h_ref, tw_ref):
    for b in range(8):
        @pl.loop(0, 4)
        def _(i):
            rows = filt_ref[pl.ds(i * 1024 + b, 128, stride=8), :]
            high = rows.astype(jnp.bfloat16)
            at = pl.ds(pl.multiple_of(i * 128, 128), 128)
            high_ref[at, lane(b)] = high
            low_ref[at, lane(b)] = (rows - high.astype(jnp.float32)).astype(jnp.bfloat16)
    stage_matmul(p_ref, table_ref, [high_ref, low_ref])

    @pl.loop(0, 512 // ROWS)
    def _(i):
        re = pl.ds(pl.multiple_of(i * ROWS, ROWS), ROWS)
        im = pl.ds(pl.multiple_of(512 + i * ROWS, ROWS), ROWS)
        points = load_points(p_ref, re, im)
        step = (step_ref[0, re, :], step_ref[1, re, :])
        turn = step
        for b in range(1, 8):
            tw_ref[re, lane(b)] = turn[0]
            tw_ref[im, lane(b)] = turn[1]
            points[b] = cmul(points[b], turn)
            if b < 7:
                turn = cmul(turn, step)
        for k2, value in enumerate(dft8(points, 1)):
            h_ref[re, lane(k2)] = value[0] * (2.0 / 8192.0)
            h_ref[im, lane(k2)] = value[1] * (2.0 / 8192.0)


def spectrum_product(p_ref, h_ref, tw_ref, g_ref):
    @pl.loop(0, 512 // ROWS)
    def _(i):
        re = pl.ds(pl.multiple_of(i * ROWS, ROWS), ROWS)
        im = pl.ds(pl.multiple_of(512 + i * ROWS, ROWS), ROWS)
        points = load_points(p_ref, re, im)
        for b in range(1, 8):
            points[b] = cmul(points[b], (tw_ref[re, lane(b)], tw_ref[im, lane(b)]))
        spec = dft8(points, 1)
        spec = [cmul(v, (h_ref[re, lane(k)], h_ref[im, lane(k)])) for k, v in enumerate(spec)]
        back = dft8(spec, -1)
        for b in range(8):
            value = back[b]
            if b > 0:
                value = cmul_conj(value, (tw_ref[re, lane(b)], tw_ref[im, lane(b)]))
            g_ref[re, lane(b)] = value[0].astype(jnp.bfloat16)
            g_ref[im, lane(b)] = value[1].astype(jnp.bfloat16)


MESH = pl.DeviceIdType.MESH


def pick_tables():
    pick = np.zeros((160, 128), np.float32)
    back = np.zeros((128, 128), np.float32)
    for b in range(-2, 8):
        for a in range(16):
            t = 8 * a + b
            if t >= 0:
                pick[(b + 2) * 16 + a, t] = 1.0
                if b >= 0:
                    back[t, b * 16 + a] = 1.0
    return pick.astype(ml_dtypes.bfloat16), back.astype(ml_dtypes.bfloat16)


class Panels:
    def __init__(self, part, sems, y, me):
        self.part, self.sems, self.y, self.me = part, sems, y, me

    def move(self, owner, kind, r, device):
        ref = self.part(owner)
        return pltpu.make_async_remote_copy(
            src_ref=ref, dst_ref=ref, send_sem=self.sems.at[kind, r - 1], recv_sem=self.sems.at[kind + 1, r - 1],
            device_id=device, device_id_type=MESH,
        )

    def across(self, r):
        return self.move(self.y, 0, r, {"lang": lax.rem(self.y + r, 4)})

    def relay(self, r):
        return self.move(lax.rem(self.y + 4 - r, 4), 0, 2, {"lang": lax.rem(self.y + r, 4)})

    def beside(self, r):
        return self.move(lax.rem(self.y + 4 - r, 4), 2, r, {"seq": lax.bitwise_xor(self.me, 1)})


def columns(d, width=LANES):
    return pl.ds(pl.multiple_of(d * width, width), width)


def tap_rows(sel_ref, rows, cols):
    return jnp.concatenate(
        [jnp.broadcast_to(sel_ref[s, pl.ds(rows[s], 1), cols], (8, LANES)) for s in range(2)], 0
    )


def short_block(pos_ref, taps, b, cols):
    total = None
    for j in range(3):
        term = pos_ref[pl.ds((b + 2 - j) * 16, 16), cols] * taps[j]
        total = term if total is None else total + term
    return total


def fused_kernel(
    lang_ref, skip_in, pick_in, unpick_in, q_in, k_in, v_in, taps_in, down_in, up_in, filt_in, table_in,
    back_in, step_in, out_ref,
    qv, kv, vv, qp, kp, vp, traw, tk_0, tk_1, tk_2, tk_3, tq_all, tsel, tqsel, down_all, up_all, down2, up2,
    halo32, halo_out, halo_in, send_x, recv_x, filt, table, back, step, high, low, p, h, tw, g, send_y, recv_y,
    qs, gate, prod, out, back_sent, skip_ref, pick_ref, unpick_ref, local_sem, halo_sem, tk_sem, tq_sem, down_sem, up_sem, x_send, x_recv, y_send, y_recv,
    out_sem, line_sem, all_sem,
):
    y = lax.axis_index("lang")
    me = lax.axis_index("seq")
    core = lax.rem(me, 2)
    tk_all = [tk_0, tk_1, tk_2, tk_3]
    loads = [
        pltpu.make_async_copy(src, dst, local_sem.at[i])
        for i, (src, dst) in enumerate([
            (taps_in, traw), (k_in.at[0], kv), (v_in.at[0], vv), (q_in.at[0], qv),
            (down_in, down_all.at[pl.ds(4 * y, 4)]), (up_in, up_all.at[pl.ds(4 * y, 4)]),
            (filt_in, filt), (table_in, table), (back_in, back), (step_in, step),
            (skip_in, skip_ref), (unpick_in, unpick_ref), (pick_in, pick_ref),
        ])
    ]
    loads[0].start()

    barrier = pltpu.get_barrier_semaphore()
    for r in range(1, 4):
        pl.semaphore_signal(barrier, inc=1, device_id={"lang": lax.rem(y + r, 4)}, device_id_type=MESH)
    for r in (1, 2, 4, 6, 8, 16, 24):
        pl.semaphore_signal(barrier, inc=1, device_id={"seq": lax.bitwise_xor(me, r)}, device_id_type=MESH)
    pl.semaphore_signal(barrier, inc=1, device_id={"seq": lax.rem(me + 31, 32)}, device_id_type=MESH)
    for load in loads[1:4] + loads[12:] + loads[4:12]:
        load.start()

    def chip_of(i, j):
        return lax.bitwise_xor(lax.div(me, 2), 4 * j + lax.bitwise_xor(j, i))

    halves = pl.ds(pl.multiple_of(core * 2048, 2048), 2048)
    chunks = [
        Panels(lambda owner, i=i: tk_all[i].at[owner], tk_sem.at[i], y, me) for i in range(4)
    ]
    tq_get = Panels(lambda owner: tq_all.at[owner, :, :, halves], tq_sem, y, me)
    down_get = Panels(lambda owner: down_all.at[pl.ds(4 * owner + 2 * core, 2)], down_sem, y, me)
    up_get = Panels(lambda owner: up_all.at[pl.ds(4 * owner + 2 * core, 2)], up_sem, y, me)

    loads[0].wait()
    for i in range(4):
        for j in range(4):
            cols = columns(chip_of(i, j), 256)
            for t in range(3):
                for n in range(2):
                    tk_all[i][y, 2 * t + n, :, 256 * j:256 * j + 256] = traw[t, n + 1, :, cols]
    for t in range(3):
        tq_all[y, t] = traw[t, 0]

    halo32[...] = jnp.zeros_like(halo32)
    for s, (load, raw) in enumerate([(loads[1], kv), (loads[2], vv), (loads[3], qv)]):
        load.wait()
        halo32[pl.ds(2 * s, 2), :] = raw[112:128, :].astype(jnp.float32)[14:16]
    halo_out[...] = halo32[...].astype(jnp.bfloat16)

    pl.semaphore_wait(barrier, 11)
    halo = pltpu.make_async_remote_copy(
        src_ref=halo_out, dst_ref=halo_in, send_sem=halo_sem.at[0], recv_sem=halo_sem.at[1],
        device_id={"seq": lax.rem(me + 1, 32)}, device_id_type=MESH,
    )
    for i, get in enumerate(chunks):
        for r in (2, 1, 3):
            get.across(r).start()
        if i == 0:
            halo.start()
    for r in (2, 4, 6):
        pl.semaphore_signal(line_sem, inc=1, device_id={"seq": lax.bitwise_xor(me, r)}, device_id_type=MESH)
    pl.semaphore_wait(line_sem, 3)
    pl.semaphore_signal(all_sem, inc=1, device_id={"seq": lax.bitwise_xor(me, 1)}, device_id_type=MESH)

    def picked(raw, pos):
        @pl.loop(0, 8)
        def _(i):
            cols = columns(i, 512)
            pos[:, cols] = jnp.dot(pick_ref[...], raw[:, cols], preferred_element_type=jnp.float32)

    def rimmed(s, pos):
        pos[pl.ds(0, 1), :] = halo32[pl.ds(2 * s, 1), :]
        pos[pl.ds(16, 1), :] = halo32[pl.ds(2 * s + 1, 1), :]

    loads[12].wait()
    picked(kv, kp)
    picked(vv, vp)
    halo.wait_recv()
    halo32[...] = jnp.where(me > 0, halo_in[...].astype(jnp.float32), 0.0)
    rimmed(0, kp)
    rimmed(1, vp)
    pl.semaphore_wait(all_sem, 1)
    owners = [lax.div(lang_ref[0, s], 4) for s in range(2)]
    places = [lax.rem(lang_ref[0, s], 4) for s in range(2)]

    def chosen(four, s):
        row = lax.broadcasted_iota(jnp.int32, four.shape, 0)
        return jnp.sum(jnp.where(row == places[s], four.astype(jnp.float32), 0.0), axis=0, keepdims=True)

    def carrier(d, tap_cols, put):
        cols = columns(d)
        taps = [[tap_rows(tsel, (2 * j + n,) * 2, tap_cols) for j in range(3)] for n in range(2)]
        for b in range(8):
            put(b, (short_block(kp, taps[0], b, cols) * short_block(vp, taps[1], b, cols)).astype(jnp.bfloat16))

    def x_copy(r):
        return pltpu.make_async_remote_copy(
            src_ref=send_x.at[r], dst_ref=recv_x.at[pl.ds(pl.multiple_of(me * 16, 16), 16), :],
            send_sem=x_send.at[r], recv_sem=x_recv.at[r],
            device_id={"seq": lax.bitwise_xor(me, r)}, device_id_type=MESH,
        )

    for i in range(4):
        for r in (1, 3, 2):
            chunks[i].across(r).wait_recv()
        for s in range(2):
            for n in range(6):
                tsel[s, pl.ds(n, 1), 1024 * i:1024 * i + 1024] = chosen(tk_all[i][owners[s], n], s)

        @pl.loop(1 if i == 0 else 0, 8)
        def _(k, i=i):
            j, flip = lax.div(k, 2), lax.rem(k, 2)
            r = 8 * j + 2 * lax.bitwise_xor(j, i) + flip

            def put(b, value):
                send_x[r, :, lane(b)] = value

            carrier(lax.bitwise_xor(me, r), columns(8 * i + 2 * j + lax.bitwise_xor(core, flip)), put)
            x_copy(r).start()

        if i == 2:
            loads[4].wait()
            for get in (tq_get, down_get):
                for r in (2, 1, 3) if get is tq_get else (1, 3):
                    get.across(r).start()

    loads[5].wait()
    for r in (3, 1):
        up_get.across(r).start()
    own = pl.ds(pl.multiple_of(me * 16, 16), 16)

    def put_own(b, value):
        recv_x[own, lane(b)] = value

    carrier(me, columns(core), put_own)
    picked(qv, qp)
    rimmed(2, qp)

    for load in loads[6:12]:
        load.wait()
    filter_spectrum(filt, table, step, high, low, p, h, tw)
    for n in range(16):
        rows = pl.ds(pl.multiple_of(32 * chip_of(n // 4, n % 4), 32), 32)
        back_sent[32 * n:32 * n + 32, :] = back[rows, :]

    down_get.across(1).wait_recv()
    down_get.relay(1).start()
    down_get.beside(1).start()

    @pl.loop(1, 32)
    def _(r):
        x_copy(r).wait_recv()

    stage_matmul(p, table, [recv_x])
    spectrum_product(p, h, tw, g)
    skip = skip_ref[pl.ds(me, 1), :]

    def y_copy(r):
        d = lax.bitwise_xor(me, r)
        j = lax.div(r, 8)
        i = lax.bitwise_xor(lax.rem(lax.div(r, 2), 4), j)
        slot = 8 * i + 2 * j + lax.rem(d, 2)
        return pltpu.make_async_remote_copy(
            src_ref=send_y.at[pl.ds(pl.multiple_of(slot * 16, 16), 16), :], dst_ref=recv_y.at[me],
            send_sem=y_send.at[r], recv_sem=y_recv.at[r],
            device_id={"seq": d}, device_id_type=MESH,
        )

    for i, group in ((0, 2), (2, 2)):
        @pl.loop(0, 1)
        def _(m, i=i):
            cols = columns(m, 1024)
            both = jnp.concatenate([skip] * 8, 1)
            conv = jnp.dot(
                back_sent[128 * i:128 * (i + group), :], g[:, cols], preferred_element_type=jnp.float32
            )
            for n in range(4 * group):
                rows = pl.ds(pl.multiple_of(32 * chip_of(i + n // 4, n % 4), 32), 32)
                send_y[128 * i + 32 * n:128 * i + 32 * n + 32, cols] = (
                    conv[32 * n:32 * n + 32] + both * recv_x[rows, cols].astype(jnp.float32)
                ).astype(jnp.bfloat16)

        @pl.loop(8 * i + (1 if i == 0 else 0), 8 * (i + group))
        def _(k):
            n, j, flip = lax.div(k, 8), lax.rem(lax.div(k, 2), 4), lax.rem(k, 2)
            y_copy(8 * j + 2 * lax.bitwise_xor(j, n) + flip).start()

    up_get.across(3).wait_recv()
    up_get.relay(3).start()
    up_get.beside(3).start()
    for r in (1, 3, 2):
        tq_get.across(r).wait_recv()
        tq_get.beside(r).start()
    down_get.across(3).wait_recv()
    down_get.beside(3).start()
    up_get.across(1).wait_recv()
    up_get.beside(1).start()
    for r in (1, 3, 2):
        tq_get.beside(r).wait_recv()
    for s in range(2):
        for t in range(3):
            tqsel[s, pl.ds(t, 1), :] = chosen(tq_all[owners[s], t], s)

    @pl.loop(0, 32)
    def _(d):
        cols = columns(d)
        taps = [tap_rows(tqsel, (j, j), cols) for j in range(3)]
        for b in range(8):
            qs[pl.ds(b * 16, 16), cols] = short_block(qp, taps, b, cols).astype(jnp.bfloat16)

    for get in (down_get, up_get):
        get.across(2).wait_recv()
        get.beside(2).start()
    for get in (down_get, up_get):
        for r in (1, 3, 2):
            get.beside(r).wait_recv()
    for s in range(2):
        down2[pl.ds(16 * s, 16), :] = down_all[lang_ref[0, s]]
        up2[pl.ds(16 * s, 16), :] = up_all[lang_ref[0, s]]
    lows = lax.dot_general(
        qs[...], down2[...], (((1,), (1,)), ((), ())), preferred_element_type=jnp.float32
    )
    row_seg = lax.rem(lax.div(lax.broadcasted_iota(jnp.int32, (128, 32), 0), 8), 2)
    col_seg = lax.div(lax.broadcasted_iota(jnp.int32, (128, 32), 1), 16)
    lows = jnp.where(row_seg == col_seg, lows, 0.0).astype(jnp.bfloat16)

    @pl.loop(0, 8)
    def _(i):
        cols = columns(i, 512)
        gate[:, cols] = qs[:, cols].astype(jnp.float32) + jnp.dot(
            lows, up2[:, cols], preferred_element_type=jnp.float32
        )

    recv_y[me] = send_y[pl.ds(pl.multiple_of(core * 16, 16), 16), :]

    halo.wait_send()
    for get in chunks + [tq_get]:
        for r in (1, 2, 3):
            get.across(r).wait_send()
    for r in (1, 2, 3):
        tq_get.beside(r).wait_send()
    for get, way in ((down_get, 1), (up_get, 3)):
        for r in (1, 3):
            get.across(r).wait_send()
        get.relay(way).wait_send()
        for r in (1, 2, 3):
            get.beside(r).wait_send()

    @pl.loop(1, 32)
    def _(r):
        x_copy(r).wait_send()

    def out_copy(i):
        cols = columns(i, 256)
        return pltpu.make_async_copy(out.at[:, cols], out_ref.at[0, :, cols], out_sem.at[i])

    @pl.loop(0, 16)
    def _(k):
        n, j = lax.div(k, 4), lax.rem(k, 4)
        r = 8 * j + 2 * lax.bitwise_xor(j, n)
        chip = lax.bitwise_xor(lax.div(me, 2), lax.div(r, 2))
        cols = columns(chip, 256)

        @pl.when(k > 0)
        def _():
            y_copy(r).wait_recv()

        y_copy(r + 1).wait_recv()
        for one in range(2):
            s = 2 * chip + one
            for b in range(8):
                piece = gate[pl.ds(b * 16, 16), columns(s)] * recv_y[s, :, lane(b)].astype(jnp.float32)
                prod[pl.ds(b * 16, 16), lane(one)] = piece.astype(jnp.bfloat16)
        out[:, cols] = jnp.dot(
            unpick_ref[...], prod[...], preferred_element_type=jnp.float32
        ).astype(jnp.bfloat16)
        out_copy(chip).start()

        @pl.when(k > 0)
        def _():
            y_copy(r).wait_send()

        y_copy(r + 1).wait_send()

    @pl.loop(0, 16)
    def _(i):
        out_copy(i).wait()


def local(q_stream, k_stream, v_stream, lang_ids, short_taps, adapter_down, adapter_up, long_filter, bypass_coefficient):
    fwd, back, step = dft_tables()
    pick, unpick = pick_tables()
    bf16, f32 = jnp.bfloat16, jnp.float32
    anywhere = pl.BlockSpec(memory_space=pl.ANY)
    dma = pltpu.SemaphoreType.DMA
    arrays = [
        ((128, 4096), bf16), ((128, 4096), bf16), ((128, 4096), bf16),
        ((160, 4096), f32), ((160, 4096), f32), ((160, 4096), f32),
        ((3, 3, 4, 4096), bf16), ] + [((4, 6, 4, 1024), bf16)] * 4 + [((4, 3, 4, 4096), bf16),
        ((2, 8, 4096), f32), ((2, 8, 4096), f32),
        ((16, 16, 4096), bf16), ((16, 16, 4096), bf16), ((32, 4096), bf16), ((32, 4096), bf16),
        ((8, 4096), f32), ((8, 4096), bf16), ((8, 4096), bf16),
        ((32, 16, 1024), bf16), ((512, 1024), bf16),
        ((4096, 128), f32), ((1024, 512), bf16), ((512, 1024), bf16), ((2, 512, 128), f32),
        ((512, 1024), bf16), ((512, 1024), bf16),
        ((1024, 1024), f32), ((1024, 1024), f32), ((1024, 1024), f32), ((1024, 1024), bf16),
        ((512, 1024), bf16), ((32, 16, 1024), bf16),
        ((128, 4096), bf16), ((128, 4096), f32), ((128, 256), bf16), ((128, 4096), bf16), ((512, 1024), bf16),
        ((32, 128), f32), ((160, 128), bf16), ((128, 128), bf16),
    ]
    return pl.pallas_call(
        fused_kernel,
        out_shape=jax.ShapeDtypeStruct(q_stream.shape, bf16),
        in_specs=[pl.BlockSpec(memory_space=pltpu.SMEM)] + [anywhere] * 13,
        out_specs=anywhere,
        scratch_shapes=[pltpu.VMEM(shape, kind) for shape, kind in arrays]
        + [dma((13,)), dma((2,)), dma((4, 4, 3)), dma((4, 3)), dma((4, 3)), dma((4, 3))]
        + [dma((32,))] * 4
        + [dma((16,)), pltpu.SemaphoreType.REGULAR, pltpu.SemaphoreType.REGULAR],
        compiler_params=pltpu.CompilerParams(
            collective_id=0, has_side_effects=True, vmem_limit_bytes=60 << 20
        ),
    )(
        lang_ids, bypass_coefficient.reshape(32, 128), jnp.asarray(pick), jnp.asarray(unpick),
        q_stream, k_stream, v_stream, short_taps.transpose(1, 2, 0, 3), adapter_down, adapter_up, long_filter,
        jnp.asarray(fwd), jnp.asarray(back), jnp.asarray(step),
    )


def solution(mesh):
    placed = (
        P("lang", "seq", None),
        P("lang", "seq", None),
        P("lang", "seq", None),
        P("lang", "seq"),
        P("lang", None, None, None),
        P("lang", None, None),
        P("lang", None, None),
        P(None, "seq"),
        P(),
    )
    return jax.shard_map(
        local, mesh=mesh, in_specs=placed, out_specs=P("lang", "seq", None), check_vma=False
    )
```
